32 devices in a mesh: days: 2 (over y), chan: 8 (over z, x), win: 2 (over core).
Axes of the slice: x: 2, y: 2, z: 4, core: 2. Of those that a mesh axis runs over, the one named last changes fastest.
Arguments:
- records: bfloat16 [2048, 2, 3000], P(('days', 'chan'), 'win'), parts along dimension 0, may hold values from -6 to 6
- assign: int32 [1024], P('chan'), may hold values from 0 to 127, as said below
- plan: int32 [1], replicated, may hold values from 0 to 2
- seg_mask: int32 [16, 2], P(('days', 'chan'), 'win'), parts along dimension 0, may hold values 0 or 1
Outputs:
- correlations: float32 [2, 1024, 128, 64], P('days', 'chan', 'win'), parts along dimension 0
The draws below stay inside these ranges and needn't reach their ends.
There are 2 independent parts, one for each index of `days`. The reference program is written for one: setup_inputs(seed, part) draws one part's arguments, and reference() takes and returns one part's arrays. A program takes and returns all parts, laid end to end along the dimension named above; an argument that names none is the same for every part. Nothing has to cross between parts.
Inputs may be any that keep to these rules, and one draw needn't show every extreme that they name: `assign`: each aligned group of 128 entries holds every number from 0 to 127 once.
All inputs are finite; a program needn't handle non-finite values. No bound on the sum of `seg_mask` on one device may be relied on, other than what follows from the above.
Results may differ from the reference program's by a relative error of at most 0.005.
Values may be sent and summed in bfloat16 or wider, within the bound.
No kernel may reach another device: no remote copies, remote signals or barrier semaphores. Data moves between devices by JAX's collectives and lax.ppermute only.
A program may use at most 64 MiB of HBM per device.

```python
import jax
import jax.numpy as jnp
from jax import lax

BLOCK_CH = 128
SEG_LEN = 3000
LAGS = 64
SEG_DEV = 1
ROUNDS = 1
BLOCKS = 8
CHANNELS = 1024
SEGMENTS = 2
CHAN_BITS = 3
N_WIN = 2


def draw_assign(key, part):
    sub_keys = jax.random.split(jax.random.fold_in(key, 17), BLOCKS)
    shuffles = jax.vmap(lambda one_key: jax.random.permutation(one_key, BLOCK_CH))(sub_keys)
    return shuffles.reshape(-1).astype(jnp.int32)


def set_ends(array, stream_key, least, top_value):
    index_at = [jax.random.randint(jax.random.fold_in(stream_key, axis), (), 0, length) for axis, length in enumerate(array.shape)]
    longest = array.shape.index(max(array.shape))
    neighbour = index_at[:longest] + [(index_at[longest] + 1) % array.shape[longest]] + index_at[longest + 1:]
    return array.at[tuple(index_at)].set(least).at[tuple(neighbour)].set(top_value)


def levels(key, shape, cuts, smallest, high):
    def one(dim, blocks):
        steps = jax.random.uniform(jax.random.fold_in(jax.random.fold_in(key, 6), dim), (blocks,), jnp.float32, smallest / len(cuts), high / len(cuts))
        return jnp.repeat(jnp.exp(steps), shape[dim] // blocks).reshape((-1,) + (1,) * (len(shape) - dim - 1))

    loudness = one(*cuts[0])
    for cut in cuts[1:]:
        loudness = loudness * one(*cut)
    return loudness


def normal_values(rng, shape, deviation, reach, pieces=(), kind=jnp.bfloat16):
    entries = deviation * jax.random.normal(rng, shape, jnp.float32)
    if pieces:
        entries = entries * levels(rng, shape, pieces, -0.22, 0.18)
    return jnp.clip(entries, -reach, reach).astype(kind)


def setup_inputs(seed: int = 0, part: int = 0) -> dict:
    key_list = jax.random.split(jax.random.key(seed), 5)
    part_keys = jax.random.split(jax.random.fold_in(key_list[4], part), 5)
    records = normal_values(part_keys[0], (CHANNELS, SEGMENTS, SEG_LEN), 1.0, 6.0, ((0, 8), (1, 2)))
    assign = draw_assign(jax.random.fold_in(key_list[4], 71), part)
    plan = jax.random.randint(key_list[2], (ROUNDS,), 0, CHAN_BITS).astype(jnp.int32)
    seg_mask = set_ends((jax.random.randint(part_keys[3], (BLOCKS, SEGMENTS), 0, 4) < 3).astype(jnp.int32), jax.random.fold_in(part_keys[3], 1), 0, 1)
    return dict(records=records, assign=assign, plan=plan, seg_mask=seg_mask)


def correlate_pair(own_block, partner_block, mask_own, mask_partner):
    own_f = own_block.astype(jnp.float32) * mask_own[None, :, None]
    partner_f = partner_block.astype(jnp.float32) * mask_partner[None, :, None]
    lag_half = LAGS // 2
    padded = jnp.pad(partner_f, ((0, 0), (0, 0), (lag_half, lag_half)))
    own_split = own_f.reshape(BLOCK_CH, N_WIN, SEG_DEV, SEG_LEN)

    def lag_term(lag_pos):
        shifted = lax.dynamic_slice_in_dim(padded, lag_pos, SEG_LEN, 2)
        shifted = shifted.reshape(BLOCK_CH, N_WIN, SEG_DEV, SEG_LEN)
        return jnp.einsum('iwst,jwst->wij', own_split, shifted)
    lag_terms = lax.map(lag_term, jnp.arange(LAGS, dtype=jnp.int32))
    rounded = lax.optimization_barrier(lag_terms.astype(jnp.bfloat16)).astype(jnp.float32)
    stacked = lax.optimization_barrier(jnp.sum(rounded, axis=1))
    valid_count = jnp.sum(mask_own * mask_partner)
    normed = stacked / (jnp.maximum(valid_count, 1.0) * jnp.sqrt(jnp.float32(SEG_LEN)))
    return jnp.transpose(normed, (1, 2, 0))

def reference(records, assign, plan, seg_mask):
    blocked = records.reshape(BLOCKS, BLOCK_CH, SEGMENTS, SEG_LEN)
    slots = assign.reshape(BLOCKS, BLOCK_CH).astype(jnp.int32)
    ordered = jnp.take_along_axis(blocked, slots[:, :, None, None], axis=1)
    masks = seg_mask.astype(jnp.float32)
    block_ids = jnp.arange(BLOCKS, dtype=jnp.int32)
    results = []
    for round_num in range(ROUNDS):
        flip = jnp.left_shift(jnp.int32(1), plan[round_num].astype(jnp.int32)).astype(jnp.int32)
        partners = jnp.bitwise_xor(block_ids, flip).astype(jnp.int32)

        def one_block(block_num):
            partner = partners[block_num]
            return correlate_pair(ordered[block_num], ordered[partner], masks[block_num], masks[partner])
        per_block = lax.map(one_block, block_ids)
        results.append(per_block.reshape(CHANNELS, BLOCK_CH, LAGS))
    return jnp.stack(results, 0)
```

```python
import math

import jax
import jax.numpy as jnp
from jax import lax
from jax.experimental import pallas as pl
from jax.experimental.pallas import tpu as pltpu
from jax.sharding import PartitionSpec as P

LAGS = 64
HALF = LAGS // 2
GROUP = 16
VMEM_BYTES = 40 * 1024 * 1024


def prep_body(win_ref, mask_ref, rec_ref, assign_ref, same_ref, cross_ref, own_ref, pad_ref, pick_ref):
    seg_len, chans = rec_ref.shape
    width = same_ref.shape[1]
    half = same_ref.shape[0]
    mask = mask_ref[0].astype(jnp.float32)
    source = lax.broadcasted_iota(jnp.int32, (chans, chans), 0)
    pick = jnp.where(source == assign_ref[...], mask, 0.0)
    pick_ref[...] = pick.T
    rec = rec_ref[...]
    pad_ref[pl.ds(0, HALF), :] = jnp.zeros((HALF, chans), jnp.bfloat16)
    pad_ref[pl.ds(HALF, seg_len), :] = rec
    tail = width - HALF - seg_len
    pad_ref[pl.ds(HALF + seg_len, tail), :] = jnp.zeros((tail, chans), jnp.bfloat16)
    win = win_ref[0]
    last = lax.broadcasted_iota(jnp.int32, (half, 128), 1) == 127
    for out_ref, start in ((same_ref, win * half), (cross_ref, (1 - win) * half)):
        rows = pick_ref[pl.ds(pl.multiple_of(start, half), half), :].astype(jnp.bfloat16)
        turned = lax.dot_general(
            rows, pad_ref[...], (((1,), (1,)), ((), ())), preferred_element_type=jnp.float32
        )
        out_ref[:, pl.ds(0, width - 128)] = turned[:, : width - 128].astype(jnp.bfloat16)
        out_ref[:, pl.ds(width - 128, 128)] = jnp.where(last, mask, turned[:, width - 128 :]).astype(
            jnp.bfloat16
        )
    ordered = jnp.dot(rec, pick.astype(jnp.bfloat16), preferred_element_type=jnp.float32)
    own_ref[pl.ds(0, seg_len), :] = ordered.astype(jnp.bfloat16)
    own_ref[pl.ds(seg_len, width - seg_len), :] = jnp.zeros((width - seg_len, chans), jnp.bfloat16)
    own_ref[pl.ds(width, 16), :] = jnp.full((16, chans), mask, jnp.float32).astype(jnp.bfloat16)


def fill_rhs(own_ref, rhs_ref):
    width, wide = rhs_ref.shape
    chans = wide // 2
    rhs_ref[:, pl.ds(0, chans)] = own_ref[pl.ds(0, width), :]
    rhs_ref[pl.ds(0, HALF), pl.ds(chans, chans)] = jnp.zeros((HALF, chans), jnp.bfloat16)
    rhs_ref[pl.ds(HALF, width - HALF), pl.ds(chans, chans)] = own_ref[pl.ds(0, width - HALF), :]


def correlate(part_ref, rhs_ref, lhs_ref):
    part = part_ref[...]
    width = part.shape[1]
    for lag in range(HALF):
        moved = part if lag == 0 else pltpu.roll(part, width - lag, 1)
        lhs_ref[pl.ds(lag * GROUP, GROUP), :] = moved
    return jnp.dot(lhs_ref[...], rhs_ref[...], preferred_element_type=jnp.float32)


def first_body(own_ref, part_ref, term_ref, rhs_ref, lhs_ref):
    @pl.when(pl.program_id(0) == 0)
    def _():
        fill_rhs(own_ref, rhs_ref)

    term_ref[...] = correlate(part_ref, rhs_ref, lhs_ref).astype(jnp.bfloat16)


def second_body(mask_ref, own_ref, part_ref, meta_ref, term_ref, out_ref, rhs_ref, lhs_ref):
    @pl.when(pl.program_id(0) == 0)
    def _():
        fill_rhs(own_ref, rhs_ref)

    width, wide = rhs_ref.shape
    chans = wide // 2
    seg_len = mask_ref[1].astype(jnp.float32)
    here = mask_ref[0].astype(jnp.float32) * meta_ref[:, pl.ds(127, 1)].astype(jnp.float32)
    there = own_ref[pl.ds(width, 16), pl.ds(0, 1)].astype(jnp.float32) * part_ref[
        :, pl.ds(width - 1, 1)
    ].astype(jnp.float32)
    scale = 1.0 / (jnp.maximum(here + there, 1.0) * jnp.sqrt(seg_len))
    scale = jnp.broadcast_to(scale, (GROUP, chans))
    terms = correlate(part_ref, rhs_ref, lhs_ref).astype(jnp.bfloat16).astype(jnp.float32)
    for lag in range(HALF):
        for high in range(2):
            rows = pl.ds(lag * GROUP, GROUP)
            lanes = pl.ds(high * chans, chans)
            mine = terms[lag * GROUP : (lag + 1) * GROUP, high * chans : (high + 1) * chans]
            total = (mine + term_ref[rows, lanes].astype(jnp.float32)) * scale
            out_ref[pl.ds(high * HALF + lag, GROUP, stride=LAGS), :] = total


def body(records, assign, plan, seg_mask):
    chans, seg_count, seg_len = records.shape
    half = chans // lax.axis_size("win")
    width = -(-(seg_len + LAGS) // 256) * 256
    win = lax.axis_index("win").astype(jnp.int32).reshape(1)
    mask = seg_mask.reshape(1)
    rec = records.reshape(chans, seg_count * seg_len).T
    bf16 = jnp.bfloat16
    smem = pl.BlockSpec(memory_space=pltpu.SMEM)
    params = pltpu.CompilerParams(vmem_limit_bytes=VMEM_BYTES)
    same, cross, own = pl.pallas_call(
        prep_body,
        out_shape=(
            jax.ShapeDtypeStruct((half, width), bf16),
            jax.ShapeDtypeStruct((half, width), bf16),
            jax.ShapeDtypeStruct((width + 16, chans), bf16),
        ),
        in_specs=[smem, smem, pl.BlockSpec(), pl.BlockSpec()],
        scratch_shapes=[pltpu.VMEM((width, chans), bf16), pltpu.VMEM((chans, chans), jnp.float32)],
        compiler_params=params,
        name="prep",
    )(win, mask, rec, assign.reshape(1, chans))

    other = lax.ppermute(own, "win", [(0, 1), (1, 0)])
    steps = half // GROUP
    rows = GROUP * HALF
    flops = 2 * half * HALF * width * 2 * chans
    scratch = [pltpu.VMEM((width, 2 * chans), bf16), pltpu.VMEM((rows, width), bf16)]
    own_spec = pl.BlockSpec((width + 16, chans), lambda s: (0, 0))
    part_spec = pl.BlockSpec((GROUP, width), lambda s: (s, 0))
    meta_spec = pl.BlockSpec((GROUP, 128), lambda s: (0, width // 128 - 1))
    term_spec = pl.BlockSpec((rows, 2 * chans), lambda s: (s, 0))
    first = pl.pallas_call(
        first_body,
        grid=(steps,),
        out_shape=jax.ShapeDtypeStruct((steps * rows, 2 * chans), bf16),
        in_specs=[own_spec, part_spec],
        out_specs=term_spec,
        scratch_shapes=scratch,
        compiler_params=params,
        cost_estimate=pl.CostEstimate(flops=flops, bytes_accessed=4 << 20, transcendentals=0),
        name="first",
    )
    second = pl.pallas_call(
        second_body,
        grid=(steps,),
        out_shape=jax.ShapeDtypeStruct((half * LAGS, chans), jnp.float32),
        in_specs=[smem, own_spec, part_spec, meta_spec, term_spec],
        out_specs=pl.BlockSpec((GROUP * LAGS, chans), lambda s: (s, 0)),
        scratch_shapes=scratch,
        compiler_params=params,
        cost_estimate=pl.CostEstimate(flops=flops, bytes_accessed=6 << 20, transcendentals=0),
        name="second",
    )
    blocks = lax.axis_size("chan")

    def exchange(bit):
        straight = []
        crossed = []
        for low in range(blocks):
            for core in range(2):
                straight.append((low * 2 + core, (low ^ 1 << bit) * 2 + core))
                crossed.append((low * 2 + core, (low ^ 1 << bit) * 2 + 1 - core))

        def run(same, cross, own):
            near = lax.ppermute(same, ("chan", "win"), straight)
            far = lax.ppermute(cross, ("chan", "win"), crossed)
            return near, far, first(own, near)

        return run

    digits = blocks.bit_length() - 1
    near, far, terms = lax.switch(plan[0], [exchange(bit) for bit in range(digits)], same, cross, own)
    scalars = jnp.concatenate([mask, jnp.full((1,), seg_len, jnp.int32)])
    out = second(scalars, other, far, near, terms)
    return jnp.transpose(out.reshape(half, LAGS, chans), (2, 0, 1))[None]


def solution(mesh):
    placed = (P(("days", "chan"), "win", None), P("chan"), P(), P(("days", "chan"), "win"))
    return jax.shard_map(
        body, mesh=mesh, in_specs=placed, out_specs=P("days", "chan", "win", None), check_vma=False
    )
```

```python
import jax
import jax.numpy as jnp
from jax import lax
from jax.experimental import pallas as pl
from jax.experimental.pallas import tpu as pltpu
from jax.sharding import PartitionSpec as P


LAGS = 64
HALF = LAGS // 2
GROUP = 16
BF16 = jnp.bfloat16
F32 = jnp.float32
PARAMS = pltpu.CompilerParams(vmem_limit_bytes=24 * 1024 * 1024)
SMEM = pl.BlockSpec(memory_space=pltpu.SMEM)
VMEM = pl.BlockSpec(memory_space=pltpu.VMEM)
ANY = pl.BlockSpec(memory_space=pl.ANY)


def picks(assign, mask, chans):
    source = lax.broadcasted_iota(jnp.int32, (chans, chans), 0)
    return jnp.where(source == assign, mask, 0.0)


def store_turned(rows, pad_ref, mask, out_refs):
    turned = lax.dot_general(
        rows.astype(BF16), pad_ref[...], (((1,), (1,)), ((), ())), preferred_element_type=F32
    )
    width = turned.shape[1]
    last = lax.broadcasted_iota(jnp.int32, (GROUP, 128), 1) == 127
    for at, out_ref in enumerate(out_refs):
        part = turned[at * GROUP : (at + 1) * GROUP]
        out_ref[:, pl.ds(0, width - 128)] = part[:, : width - 128].astype(BF16)
        out_ref[:, pl.ds(width - 128, 128)] = jnp.where(last, mask, part[:, width - 128 :]).astype(BF16)


def near_body(win_ref, mask_ref, rec_ref, assign_ref, *refs):
    out_refs = refs[:-4]
    pad_ref, pick_ref, slot_ref, sem = refs[-4:]
    seg_len, chans = rec_ref.shape
    width = pad_ref.shape[0]
    half = GROUP * len(out_refs)
    tail = width - HALF - seg_len
    load = pltpu.make_async_copy(rec_ref, pad_ref.at[pl.ds(HALF, seg_len)], sem.at[0])
    slots = pltpu.make_async_copy(assign_ref, slot_ref, sem.at[1])
    slots.start()
    load.start()
    pad_ref[pl.ds(0, HALF), :] = jnp.zeros((HALF, chans), BF16)
    pad_ref[pl.ds(HALF + seg_len, tail), :] = jnp.zeros((tail, chans), BF16)
    mask = mask_ref[0].astype(F32)
    slots.wait()
    pick_ref[...] = picks(slot_ref[...], mask, chans).T
    start = pl.multiple_of(win_ref[0] * half, half)
    rows = pick_ref[pl.ds(start, half), :]
    load.wait()
    store_turned(rows, pad_ref, mask, out_refs)


def far_body(win_ref, mask_ref, rec_ref, assign_ref, own_ref, *refs):
    out_refs = refs[:-4]
    pad_ref, pick_ref, slot_ref, sem = refs[-4:]
    seg_len, chans = rec_ref.shape
    width = pad_ref.shape[0]
    half = GROUP * len(out_refs)
    tail = width - HALF - seg_len
    load = pltpu.make_async_copy(rec_ref, pad_ref.at[pl.ds(HALF, seg_len)], sem.at[0])
    slots = pltpu.make_async_copy(assign_ref, slot_ref, sem.at[1])
    slots.start()
    load.start()
    pad_ref[pl.ds(0, HALF), :] = jnp.zeros((HALF, chans), BF16)
    pad_ref[pl.ds(HALF + seg_len, tail), :] = jnp.zeros((tail, chans), BF16)
    mask = mask_ref[0].astype(F32)
    slots.wait()
    pick = picks(slot_ref[...], mask, chans)
    pick_ref[...] = pick.T
    start = pl.multiple_of((1 - win_ref[0]) * half, half)
    rows = pick_ref[pl.ds(start, half), :]
    load.wait()
    store_turned(rows, pad_ref, mask, out_refs)
    ordered = jnp.dot(pad_ref[...], pick.astype(BF16), preferred_element_type=F32)
    own_ref[pl.ds(0, width), :] = ordered.astype(BF16)
    own_ref[pl.ds(width, HALF), :] = jnp.zeros((HALF, chans), BF16)
    own_ref[pl.ds(width + HALF, 16), :] = jnp.full((16, chans), mask, F32).astype(BF16)


def correlate(part_ref, own_ref, lhs_ref):
    part = part_ref[...]
    width = part.shape[1]
    for lag in range(HALF):
        moved = part if lag == 0 else pltpu.roll(part, width - lag, 1)
        lhs_ref[pl.ds(lag * GROUP, GROUP), :] = moved
    rhs = jnp.concatenate([own_ref[pl.ds(HALF, width), :], own_ref[pl.ds(0, width), :]], axis=1)
    return jnp.dot(lhs_ref[...], rhs, preferred_element_type=F32)


def first_body(own_ref, part_ref, term_ref, lhs_ref):
    term_ref[...] = correlate(part_ref, own_ref, lhs_ref).astype(BF16)


def second_body(at, mask_ref, own_ref, part_ref, near_ref, term_ref, *refs):
    out_ref, lhs_ref, done_ref, sem = refs[-4:]
    width = part_ref.shape[1]
    chans = own_ref.shape[1]
    seg_len = mask_ref[1].astype(F32)
    here = mask_ref[0].astype(F32) * near_ref[:, pl.ds(width - 1, 1)].astype(F32)
    there = own_ref[pl.ds(width + HALF, GROUP), pl.ds(0, 1)].astype(F32) * part_ref[
        :, pl.ds(width - 1, 1)
    ].astype(F32)
    scale = 1.0 / (jnp.maximum(here + there, 1.0) * jnp.sqrt(seg_len))
    scale = jnp.broadcast_to(scale, (GROUP, chans))
    terms = correlate(part_ref, own_ref, lhs_ref).astype(BF16).astype(F32)
    for lag in range(HALF):
        for high in range(2):
            rows = pl.ds(lag * GROUP, GROUP)
            lanes = pl.ds(high * chans, chans)
            mine = terms[lag * GROUP : (lag + 1) * GROUP, high * chans : (high + 1) * chans]
            total = (mine + term_ref[rows, lanes].astype(F32)) * scale
            done_ref[pl.ds(high * HALF + lag, GROUP, stride=LAGS), :] = total
    count = GROUP * LAGS
    store = pltpu.make_async_copy(done_ref, out_ref.at[pl.ds(at * count, count)], sem)
    store.start()
    store.wait()


def body(records, assign, plan, seg_mask):
    chans, seg_count, seg_len = records.shape
    blocks = lax.axis_size("chan")
    half = chans // lax.axis_size("win")
    groups = half // GROUP
    width = -(-(seg_len + LAGS) // 256) * 256
    win = lax.axis_index("win").astype(jnp.int32).reshape(1)
    mask = seg_mask.reshape(1)
    rec = records.reshape(chans, seg_count * seg_len).T
    slots = assign.reshape(1, chans)
    scalars = jnp.concatenate([mask, jnp.full((1,), seg_len, jnp.int32)])
    piece = jax.ShapeDtypeStruct((GROUP, width), BF16)
    prep_scratch = [
        pltpu.VMEM((width, chans), BF16),
        pltpu.VMEM((chans, chans), F32),
        pltpu.VMEM((1, chans), jnp.int32),
        pltpu.SemaphoreType.DMA((2,)),
    ]
    near_prep = pl.pallas_call(
        near_body,
        out_shape=(piece,) * groups,
        in_specs=[SMEM, SMEM, ANY, ANY],
        out_specs=(VMEM,) * groups,
        scratch_shapes=prep_scratch,
        compiler_params=PARAMS,
        cost_estimate=pl.CostEstimate(flops=1 << 26, bytes_accessed=1 << 20, transcendentals=0),
        name="near_prep",
    )
    own_shape = (width + HALF + 16, chans)
    far_prep = pl.pallas_call(
        far_body,
        out_shape=(jax.ShapeDtypeStruct(own_shape, BF16),) + (piece,) * groups,
        in_specs=[SMEM, SMEM, ANY, ANY],
        out_specs=(VMEM,) * (groups + 1),
        scratch_shapes=prep_scratch,
        compiler_params=PARAMS,
        cost_estimate=pl.CostEstimate(flops=1 << 27, bytes_accessed=1 << 20, transcendentals=0),
        name="far_prep",
    )
    rows = GROUP * HALF
    flops = 2 * rows * width * 2 * chans
    lhs = pltpu.VMEM((rows, width), BF16)
    first = pl.pallas_call(
        first_body,
        out_shape=jax.ShapeDtypeStruct((rows, 2 * chans), BF16),
        in_specs=[VMEM, VMEM],
        out_specs=VMEM,
        scratch_shapes=[lhs],
        compiler_params=PARAMS,
        cost_estimate=pl.CostEstimate(flops=flops, bytes_accessed=1 << 20, transcendentals=0),
        name="first",
    )
    total = jax.ShapeDtypeStruct((half * LAGS, chans), F32)

    def second(at):
        return pl.pallas_call(
            lambda *refs: second_body(at, *refs),
            out_shape=total,
            in_specs=[SMEM, VMEM, VMEM, VMEM, VMEM] + [ANY] * (at > 0),
            out_specs=ANY,
            scratch_shapes=[lhs, pltpu.VMEM((GROUP * LAGS, chans), F32), pltpu.SemaphoreType.DMA],
            input_output_aliases={5: 0} if at else {},
            compiler_params=PARAMS,
            cost_estimate=pl.CostEstimate(flops=flops, bytes_accessed=1 << 20, transcendentals=0),
            name="second",
        )

    def exchange(bit):
        straight = []
        crossed = []
        for low in range(blocks):
            for core in range(2):
                straight.append((low * 2 + core, (low ^ 1 << bit) * 2 + core))
                crossed.append((low * 2 + core, (low ^ 1 << bit) * 2 + 1 - core))

        def run(same):
            own, *cross = far_prep(win, mask, rec, slots)
            near = []
            for one in same:
                near.append(lax.ppermute(one, ("chan", "win"), straight))
            far = []
            for one in cross:
                far.append(lax.ppermute(one, ("chan", "win"), crossed))
            other = lax.ppermute(own, "win", [(0, 1), (1, 0)])
            out = ()
            for at in range(groups):
                terms = first(own, near[at])
                out = (second(at)(scalars, other, far[at], near[at], terms, *out),)
            return out[0]

        return run

    digits = blocks.bit_length() - 1
    same = near_prep(win, mask, rec, slots)
    out = lax.switch(plan[0], [exchange(bit) for bit in range(digits)], same)
    return jnp.transpose(out.reshape(half, LAGS, chans), (2, 0, 1))[None]


def solution(mesh):
    placed = (P(("days", "chan"), "win", None), P("chan"), P(), P(("days", "chan"), "win"))
    return jax.shard_map(
        body, mesh=mesh, in_specs=placed, out_specs=P("days", "chan", "win", None), check_vma=False
    )
```

```python
import math

import jax
import jax.numpy as jnp
from jax import lax
from jax.experimental import pallas as pl
from jax.experimental.pallas import tpu as pltpu
from jax.sharding import PartitionSpec as P


LAGS = 64
HALF = LAGS // 2
GROUP = 16
NEARS = 2
LOADS = 4
BF16 = jnp.bfloat16
F32 = jnp.float32
PARAMS = pltpu.CompilerParams(vmem_limit_bytes=24 * 1024 * 1024)

NEAR_PARAMS = pltpu.CompilerParams(vmem_limit_bytes=62 * 1024 * 1024)
SMEM = pl.BlockSpec(memory_space=pltpu.SMEM)
VMEM = pl.BlockSpec(memory_space=pltpu.VMEM)
ANY = pl.BlockSpec(memory_space=pl.ANY)
HBM = pl.BlockSpec(memory_space=pltpu.HBM)


def picks(assign, mask, chans):
    source = lax.broadcasted_iota(jnp.int32, (chans, chans), 0)
    return jnp.where(source == assign, mask, 0.0)


def store_turned(rows, pad_ref, mask, out_refs):
    turned = lax.dot_general(
        rows, pad_ref[...], (((1,), (1,)), ((), ())), preferred_element_type=F32
    )
    width = turned.shape[1]
    at = 0
    for out_ref in out_refs:
        count = out_ref.shape[0]
        last = lax.broadcasted_iota(jnp.int32, (count, 128), 1) == 127
        part = turned[at : at + count]
        at += count
        out_ref[:, pl.ds(0, width - 128)] = part[:, : width - 128].astype(BF16)
        out_ref[:, pl.ds(width - 128, 128)] = jnp.where(last, mask, part[:, width - 128 :]).astype(BF16)


def near_body(win_ref, mask_ref, rec_ref, assign_ref, *refs):
    out_refs = refs[:-7]
    pad_ref, far_ref, pick_ref, meta_ref, turn_ref, slot_ref, sem = refs[-7:]
    seg_len, chans = rec_ref.shape
    width = pad_ref.shape[0]
    half = chans // 2
    tail = width - HALF - seg_len
    slots = pltpu.make_async_copy(assign_ref, slot_ref, sem.at[LOADS])
    slots.start()
    cut = -(-seg_len // (8 * LOADS)) * 8
    loads = []
    for at in range(LOADS):
        count = min(cut, seg_len - at * cut)
        source = rec_ref.at[pl.ds(at * cut, count)]
        target = pad_ref.at[pl.ds(HALF + at * cut, count)]
        loads.append(pltpu.make_async_copy(source, target, sem.at[at]))
        loads[-1].start()
    pad_ref[pl.ds(0, HALF), :] = jnp.zeros((HALF, chans), BF16)
    pad_ref[pl.ds(HALF + seg_len, tail), :] = jnp.zeros((tail, chans), BF16)
    mask = mask_ref[0, 0].astype(F32)
    meta_ref[...] = jnp.full(meta_ref.shape, mask, F32)
    slots.wait()
    pick = picks(slot_ref[...], mask, chans)
    pick_ref[...] = pick.astype(BF16)
    turn_ref[...] = pick.T
    start = pl.multiple_of(win_ref[0] * half, half)
    other = pl.multiple_of((1 - win_ref[0]) * half, half)
    rows = turn_ref[pl.ds(start, half), :]
    far_ref[...] = turn_ref[pl.ds(other, half), :].astype(BF16)
    for load in loads:
        load.wait()
    store_turned(rows.astype(BF16), pad_ref, mask, out_refs)


def far_body(pad_ref, rows_ref, pick_ref, meta_ref, own_ref, *out_refs):
    width, chans = pad_ref.shape
    mask = meta_ref[pl.ds(0, 1), pl.ds(0, 1)]
    store_turned(rows_ref[...], pad_ref, mask, out_refs)
    ordered = jnp.dot(pad_ref[...], pick_ref[...], preferred_element_type=F32)
    own_ref[pl.ds(0, width), :] = ordered.astype(BF16)
    own_ref[pl.ds(width, HALF), :] = jnp.zeros((HALF, chans), BF16)
    own_ref[pl.ds(width + HALF, 16), :] = meta_ref[...].astype(BF16)


def correlate(part, own_ref, lhs_ref):
    width = part.shape[1]
    for lag in range(HALF):
        moved = part if lag == 0 else pltpu.roll(part, width - lag, 1)
        lhs_ref[pl.ds(lag * GROUP, GROUP), :] = moved
    rhs = jnp.concatenate([own_ref[pl.ds(HALF, width), :], own_ref[pl.ds(0, width), :]], axis=1)
    return jnp.dot(lhs_ref[...], rhs, preferred_element_type=F32)


def first_body(own_ref, part_ref, term_ref, lhs_ref):
    def step(at, carry):
        part = part_ref[pl.ds(pl.multiple_of(at * GROUP, GROUP), GROUP), :]
        terms = correlate(part, own_ref, lhs_ref).astype(BF16)
        term_ref[pl.ds(pl.multiple_of(at * GROUP * HALF, GROUP), GROUP * HALF), :] = terms
        return carry

    lax.fori_loop(0, part_ref.shape[0] // GROUP, step, 0)


def second_body(at, skip, seg_len, meta_ref, own_ref, part_ref, near_ref, term_ref, *refs):
    out_ref, lhs_ref, done_ref, sem = refs[-4:]
    width = part_ref.shape[1]
    chans = own_ref.shape[1]
    here = meta_ref[...] * near_ref[pl.ds(skip, GROUP), pl.ds(width - 128, 128)].astype(F32)
    there = own_ref[pl.ds(width + HALF, GROUP), :].astype(F32) * part_ref[
        :, pl.ds(width - 128, 128)
    ].astype(F32)
    count = (here + there)[:, 127:128]
    scale = 1.0 / (jnp.maximum(count, 1.0) * math.sqrt(seg_len))
    scale = jnp.broadcast_to(scale, (GROUP, chans))
    terms = correlate(part_ref[...], own_ref, lhs_ref).astype(BF16).astype(F32)
    stores = []
    slab = 8
    for low in range(0, GROUP, slab):
        for lag in range(HALF):
            for high in range(2):
                row = lag * GROUP + low
                lanes = pl.ds(high * chans, chans)
                mine = terms[row : row + slab, high * chans : (high + 1) * chans]
                held = term_ref[pl.ds(skip * HALF + row, slab), lanes].astype(F32)
                total = (mine + held) * scale[low : low + slab]
                done_ref[pl.ds(low * LAGS + high * HALF + lag, slab, stride=LAGS), :] = total
        source = done_ref.at[pl.ds(low * LAGS, slab * LAGS)]
        target = out_ref.at[pl.ds((at * GROUP + low) * LAGS, slab * LAGS)]
        stores.append(pltpu.make_async_copy(source, target, sem.at[low // slab]))
        stores[-1].start()
    for store in stores:
        store.wait()


def body(records, assign, plan, seg_mask):
    chans, seg_count, seg_len = records.shape
    blocks = lax.axis_size("chan")
    half = chans // lax.axis_size("win")
    groups = half // GROUP
    width = -(-(seg_len + LAGS) // 256) * 256
    win = lax.axis_index("win").astype(jnp.int32).reshape(1)
    rec = records.reshape(chans, seg_count * seg_len).T
    slots = assign.reshape(1, chans)
    per_near = half // NEARS
    shape = jax.ShapeDtypeStruct
    near_prep = pl.pallas_call(
        near_body,
        out_shape=(shape((per_near, width), BF16),) * NEARS
        + (shape((width, chans), BF16), shape((half, chans), BF16), shape((chans, chans), BF16))
        + (shape((16, 128), F32),),
        in_specs=[SMEM, SMEM, HBM, HBM],
        out_specs=(VMEM,) * (NEARS + 4),
        scratch_shapes=[
            pltpu.VMEM((chans, chans), F32),
            pltpu.VMEM((1, chans), jnp.int32),
            pltpu.SemaphoreType.DMA((LOADS + 1,)),
        ],
        compiler_params=NEAR_PARAMS,
        cost_estimate=pl.CostEstimate(flops=1 << 26, bytes_accessed=1 << 20, transcendentals=0),
        name="near_prep",
    )
    far_prep = pl.pallas_call(
        far_body,
        out_shape=(shape((width + HALF + 16, chans), BF16),) + (shape((GROUP, width), BF16),) * groups,
        in_specs=[VMEM] * 4,
        out_specs=(VMEM,) * (groups + 1),
        compiler_params=PARAMS,
        cost_estimate=pl.CostEstimate(flops=1 << 27, bytes_accessed=1 << 20, transcendentals=0),
        name="far_prep",
    )
    rows = GROUP * HALF
    flops = 2 * rows * width * 2 * chans
    lhs = pltpu.VMEM((rows, width), BF16)
    first = pl.pallas_call(
        first_body,
        out_shape=shape((per_near * HALF, 2 * chans), BF16),
        in_specs=[VMEM, VMEM],
        out_specs=VMEM,
        scratch_shapes=[lhs],
        compiler_params=PARAMS,
        cost_estimate=pl.CostEstimate(flops=2 * flops, bytes_accessed=1 << 20, transcendentals=0),
        name="first",
    )

    def second(at):
        skip = at * GROUP % per_near
        return pl.pallas_call(
            lambda *refs: second_body(at, skip, seg_len, *refs),
            out_shape=shape((half * LAGS, chans), F32),
            in_specs=[VMEM] * 5 + [ANY] * (at > 0),
            out_specs=ANY,
            scratch_shapes=[lhs, pltpu.VMEM((GROUP * LAGS, chans), F32), pltpu.SemaphoreType.DMA((2,))],
            input_output_aliases={5: 0} if at else {},
            compiler_params=PARAMS,
            cost_estimate=pl.CostEstimate(flops=flops, bytes_accessed=1 << 20, transcendentals=0),
            name="second",
        )

    def exchange(bit):
        straight = []
        crossed = []
        for low in range(blocks):
            for core in range(2):
                straight.append((low * 2 + core, (low ^ 1 << bit) * 2 + core))
                crossed.append((low * 2 + core, (low ^ 1 << bit) * 2 + 1 - core))

        def run(same, pad, turned, pick, meta):
            own, *cross = far_prep(pad, turned, pick, meta)
            near = []
            for one in same:
                near.append(lax.ppermute(one, ("chan", "win"), straight))
            far = []
            for one in cross:
                far.append(lax.ppermute(one, ("chan", "win"), crossed))
            other = lax.ppermute(own, "win", [(0, 1), (1, 0)])
            terms = [first(own, one) for one in near]
            out = ()
            for at in range(groups):
                side = at * GROUP // per_near
                out = (second(at)(meta, other, far[at], near[side], terms[side], *out),)
            return out[0]

        return run

    digits = blocks.bit_length() - 1
    *same, pad, turned, pick, meta = near_prep(win, seg_mask, rec, slots)
    branches = [exchange(bit) for bit in range(digits)]
    out = lax.switch(plan[0], branches, same, pad, turned, pick, meta)
    return jnp.transpose(out.reshape(half, LAGS, chans), (2, 0, 1))[None]


def solution(mesh):
    placed = (P(("days", "chan"), "win", None), P("chan"), P(), P(("days", "chan"), "win"))
    return jax.shard_map(
        body, mesh=mesh, in_specs=placed, out_specs=P("days", "chan", "win", None), check_vma=False
    )
```

```python
import math

import jax
import jax.numpy as jnp
from jax import lax
from jax.experimental import pallas as pl
from jax.experimental.pallas import tpu as pltpu
from jax.sharding import PartitionSpec as P


LAGS = 64
HALF = LAGS // 2
GROUP = 16
NEARS = 2
LOADS = 4
FARS = (16, 16, 16, 8, 8)
BF16 = jnp.bfloat16
F32 = jnp.float32
PARAMS = pltpu.CompilerParams(vmem_limit_bytes=24 * 1024 * 1024)

NEAR_PARAMS = pltpu.CompilerParams(vmem_limit_bytes=62 * 1024 * 1024)
SMEM = pl.BlockSpec(memory_space=pltpu.SMEM)
VMEM = pl.BlockSpec(memory_space=pltpu.VMEM)
ANY = pl.BlockSpec(memory_space=pl.ANY)
HBM = pl.BlockSpec(memory_space=pltpu.HBM)


def picks(assign, mask, chans):
    source = lax.broadcasted_iota(jnp.int32, (chans, chans), 0)
    return jnp.where(source == assign, mask, 0.0)


def store_turned(rows, pad_ref, mask, out_refs):
    turned = lax.dot_general(
        rows, pad_ref[...], (((1,), (1,)), ((), ())), preferred_element_type=F32
    )
    width = turned.shape[1]
    at = 0
    for out_ref in out_refs:
        count = out_ref.shape[0]
        last = lax.broadcasted_iota(jnp.int32, (count, 128), 1) == 127
        part = turned[at : at + count]
        at += count
        out_ref[:, pl.ds(0, width - 128)] = part[:, : width - 128].astype(BF16)
        out_ref[:, pl.ds(width - 128, 128)] = jnp.where(last, mask, part[:, width - 128 :]).astype(BF16)


def near_body(win_ref, mask_ref, rec_ref, assign_ref, *refs):
    out_refs = refs[:-7]
    pad_ref, far_ref, pick_ref, meta_ref, turn_ref, slot_ref, sem = refs[-7:]
    seg_len, chans = rec_ref.shape
    width = pad_ref.shape[0]
    half = chans // 2
    tail = width - HALF - seg_len
    slots = pltpu.make_async_copy(assign_ref, slot_ref, sem.at[LOADS])
    slots.start()
    cut = -(-seg_len // (8 * LOADS)) * 8
    loads = []
    for at in range(LOADS):
        count = min(cut, seg_len - at * cut)
        source = rec_ref.at[pl.ds(at * cut, count)]
        target = pad_ref.at[pl.ds(HALF + at * cut, count)]
        loads.append(pltpu.make_async_copy(source, target, sem.at[at]))
        loads[-1].start()
    pad_ref[pl.ds(0, HALF), :] = jnp.zeros((HALF, chans), BF16)
    pad_ref[pl.ds(HALF + seg_len, tail), :] = jnp.zeros((tail, chans), BF16)
    mask = mask_ref[0, 0].astype(F32)
    meta_ref[...] = jnp.full(meta_ref.shape, mask, F32)
    slots.wait()
    pick = picks(slot_ref[...], mask, chans)
    pick_ref[...] = pick.astype(BF16)
    turn_ref[...] = pick.T
    start = pl.multiple_of(win_ref[0] * half, half)
    other = pl.multiple_of((1 - win_ref[0]) * half, half)
    rows = turn_ref[pl.ds(start, half), :]
    far_ref[...] = turn_ref[pl.ds(other, half), :].astype(BF16)
    for load in loads:
        load.wait()
    store_turned(rows.astype(BF16), pad_ref, mask, out_refs)


def far_body(pad_ref, rows_ref, pick_ref, meta_ref, own_ref, *out_refs):
    width, chans = pad_ref.shape
    mask = meta_ref[pl.ds(0, 1), pl.ds(0, 1)]
    store_turned(rows_ref[...], pad_ref, mask, out_refs)
    ordered = jnp.dot(pad_ref[...], pick_ref[...], preferred_element_type=F32)
    own_ref[pl.ds(0, width), :] = ordered.astype(BF16)
    own_ref[pl.ds(width, HALF), :] = jnp.zeros((HALF, chans), BF16)
    own_ref[pl.ds(width + HALF, 16), :] = meta_ref[...].astype(BF16)


def correlate(part, own_ref, lhs_ref):
    count, width = part.shape
    pack = GROUP // count
    for lag in range(0, HALF, pack):
        moved = [part if step == 0 else pltpu.roll(part, width - step, 1) for step in range(lag, lag + pack)]
        lhs_ref[pl.ds(lag * count, GROUP), :] = jnp.concatenate(moved, axis=0)
    rhs = jnp.concatenate([own_ref[pl.ds(HALF, width), :], own_ref[pl.ds(0, width), :]], axis=1)
    return jnp.dot(lhs_ref[...], rhs, preferred_element_type=F32)


def first_body(own_ref, part_ref, *refs):
    term_ref, lhs_ref = refs[-2:]

    def step(at, carry):
        part = part_ref[pl.ds(pl.multiple_of(at * GROUP, GROUP), GROUP), :]
        terms = correlate(part, own_ref, lhs_ref).astype(BF16)
        term_ref[pl.ds(pl.multiple_of(at * GROUP * HALF, GROUP), GROUP * HALF), :] = terms
        return carry

    lax.fori_loop(0, part_ref.shape[0] // GROUP, step, 0)


def second_body(before, row, skip, final, seg_len, meta_ref, own_ref, part_ref, near_ref, term_ref, *refs):
    lhs_ref, sem = refs[-2:]
    count, width = part_ref.shape
    chans = own_ref.shape[1]
    outs = []
    if before:
        prior_ref = refs[0]
        out_ref = refs[2] if row > before else refs[1]
        target = out_ref.at[pl.ds((row - before) * LAGS, before * LAGS)]
        outs.append(pltpu.make_async_copy(prior_ref, target, sem.at[0]))
        outs[-1].start()
    done_ref = refs[-3]
    here = meta_ref[pl.ds(0, count), :] * near_ref[pl.ds(skip, count), pl.ds(width - 128, 128)].astype(F32)
    there = own_ref[pl.ds(width + HALF, count), :].astype(F32) * part_ref[
        :, pl.ds(width - 128, 128)
    ].astype(F32)
    valid = (here + there)[:, 127:128]
    scale = 1.0 / (jnp.maximum(valid, 1.0) * math.sqrt(seg_len))
    scale = jnp.broadcast_to(scale, (count, chans))
    terms = correlate(part_ref[...], own_ref, lhs_ref).astype(BF16).astype(F32)
    slab = 8
    for low in range(0, count, slab):
        at = skip + low
        held_at = at // GROUP * GROUP * HALF + at % GROUP
        for lag in range(HALF):
            for high in range(2):
                lanes = pl.ds(high * chans, chans)
                line = lag * count + low
                mine = terms[line : line + slab, high * chans : (high + 1) * chans]
                held = term_ref[pl.ds(held_at + lag * GROUP, slab), lanes].astype(F32)
                total = (mine + held) * scale[low : low + slab]
                done_ref[pl.ds(low * LAGS + high * HALF + lag, slab, stride=LAGS), :] = total
        if final:
            source = done_ref.at[pl.ds(low * LAGS, slab * LAGS)]
            target = out_ref.at[pl.ds((row + low) * LAGS, slab * LAGS)]
            outs.append(pltpu.make_async_copy(source, target, sem.at[1 + low // slab]))
            outs[-1].start()
    for out in outs:
        out.wait()


def body(records, assign, plan, seg_mask):
    chans, seg_count, seg_len = records.shape
    blocks = lax.axis_size("chan")
    half = chans // lax.axis_size("win")
    width = -(-(seg_len + LAGS) // 256) * 256
    win = lax.axis_index("win").astype(jnp.int32).reshape(1)
    rec = records.reshape(chans, seg_count * seg_len).T
    slots = assign.reshape(1, chans)
    per_near = half // NEARS
    shape = jax.ShapeDtypeStruct
    near_prep = pl.pallas_call(
        near_body,
        out_shape=(shape((per_near, width), BF16),) * NEARS
        + (shape((width, chans), BF16), shape((half, chans), BF16), shape((chans, chans), BF16))
        + (shape((16, 128), F32),),
        in_specs=[SMEM, SMEM, HBM, HBM],
        out_specs=(VMEM,) * (NEARS + 4),
        scratch_shapes=[
            pltpu.VMEM((chans, chans), F32),
            pltpu.VMEM((1, chans), jnp.int32),
            pltpu.SemaphoreType.DMA((LOADS + 1,)),
        ],
        compiler_params=NEAR_PARAMS,
        cost_estimate=pl.CostEstimate(flops=1 << 26, bytes_accessed=1 << 20, transcendentals=0),
        name="near_prep",
    )
    far_prep = pl.pallas_call(
        far_body,
        out_shape=(shape((width + HALF + 16, chans), BF16),) + tuple(
            shape((count, width), BF16) for count in FARS
        ),
        in_specs=[VMEM] * 4,
        out_specs=(VMEM,) * (len(FARS) + 1),
        compiler_params=PARAMS,
        cost_estimate=pl.CostEstimate(flops=1 << 27, bytes_accessed=1 << 20, transcendentals=0),
        name="far_prep",
    )
    rows = GROUP * HALF
    flops = 2 * rows * width * 2 * chans
    lhs = pltpu.VMEM((rows, width), BF16)

    def first(*args):
        return pl.pallas_call(
            first_body,
            out_shape=shape((per_near * HALF, 2 * chans), BF16),
            in_specs=[VMEM, VMEM] + [ANY] * (len(args) - 2),
            out_specs=VMEM,
            scratch_shapes=[lhs],
            compiler_params=PARAMS,
            cost_estimate=pl.CostEstimate(flops=2 * flops, bytes_accessed=1 << 20, transcendentals=0),
            name="first",
        )(*args)

    def second(before, row, count):
        skip = row % per_near
        final = row + count == half
        total = shape((half * LAGS, chans), F32)
        done = shape((count * LAGS, chans), F32)
        lines = pltpu.VMEM((count * HALF, width), BF16)
        sems = pltpu.SemaphoreType.DMA((3,))
        if final:
            extra = dict(out_shape=(total,), out_specs=(ANY,))
            scratch = [pltpu.VMEM(done.shape, F32), lines, sems]
        elif before:
            extra = dict(out_shape=(total, done), out_specs=(ANY, VMEM))
            scratch = [lines, sems]
        else:
            extra = dict(out_shape=(done,), out_specs=(VMEM,))
            scratch = [lines, sems]
        return pl.pallas_call(
            lambda *refs: second_body(before, row, skip, final, seg_len, *refs),
            in_specs=[VMEM] * 5 + [VMEM] * (before > 0) + [ANY] * (row > before),
            scratch_shapes=scratch,
            input_output_aliases={6: 0} if row > before else {},
            compiler_params=PARAMS,
            cost_estimate=pl.CostEstimate(flops=flops, bytes_accessed=1 << 20, transcendentals=0),
            name="second",
            **extra,
        )

    def exchange(bit):
        straight = []
        crossed = []
        for low in range(blocks):
            for core in range(2):
                straight.append((low * 2 + core, (low ^ 1 << bit) * 2 + core))
                crossed.append((low * 2 + core, (low ^ 1 << bit) * 2 + 1 - core))

        def run(same, pad, turned, pick, meta):
            own, *cross = far_prep(pad, turned, pick, meta)
            near = []
            for one in same:
                near.append(lax.ppermute(one, ("chan", "win"), straight))
            far = []
            for one in cross:
                far.append(lax.ppermute(one, ("chan", "win"), crossed))
            other = lax.ppermute(own, "win", [(0, 1), (1, 0)])
            terms = []
            for one in near:
                terms.append(first(own, one, *terms[-1:]))
            out = done = ()
            before = row = 0
            for one in far:
                count = one.shape[0]
                side = row // per_near
                step = second(before, row, count)
                result = step(meta, other, one, near[side], terms[side], *done, *out)
                out = result[:1] if before else ()
                done = result[-1:]
                before = count
                row += count
            return out[0]

        return run

    digits = blocks.bit_length() - 1
    *same, pad, turned, pick, meta = near_prep(win, seg_mask, rec, slots)
    branches = [exchange(bit) for bit in range(digits)]
    out = lax.switch(plan[0], branches, same, pad, turned, pick, meta)
    return jnp.transpose(out.reshape(half, LAGS, chans), (2, 0, 1))[None]


def solution(mesh):
    placed = (P(("days", "chan"), "win", None), P("chan"), P(), P(("days", "chan"), "win"))
    return jax.shard_map(
        body, mesh=mesh, in_specs=placed, out_specs=P("days", "chan", "win", None), check_vma=False
    )
```

```python
import math

import jax
import jax.numpy as jnp
from jax import lax
from jax.experimental import pallas as pl
from jax.experimental.pallas import tpu as pltpu
from jax.sharding import PartitionSpec as P


LAGS = 64
HALF = LAGS // 2
GROUP = 16
NEARS = 2
LOADS = 1
FARS = (16, 16, 16, 16)
BF16 = jnp.bfloat16
F32 = jnp.float32
PARAMS = pltpu.CompilerParams(vmem_limit_bytes=24 * 1024 * 1024)

NEAR_PARAMS = pltpu.CompilerParams(vmem_limit_bytes=62 * 1024 * 1024)
SMEM = pl.BlockSpec(memory_space=pltpu.SMEM)
VMEM = pl.BlockSpec(memory_space=pltpu.VMEM)
ANY = pl.BlockSpec(memory_space=pl.ANY)
HBM = pl.BlockSpec(memory_space=pltpu.HBM)


def store_turned(rows, pad_ref, start, size, out_refs):
    turned = lax.dot_general(
        rows, pad_ref[pl.ds(start, size), :], (((1,), (1,)), ((), ())), preferred_element_type=F32
    )
    at = 0
    for out_ref in out_refs:
        count = out_ref.shape[0]
        out_ref[:, pl.ds(start, size)] = turned[at : at + count].astype(BF16)
        at += count


def near_body(win_ref, rec_ref, assign_ref, near_ref, pad_ref, rows_ref, pick_ref, turn_ref, slot_ref, sem):
    seg_len, chans = rec_ref.shape
    width = pad_ref.shape[0]
    half = chans // 2
    tail = width - HALF - seg_len
    slots = pltpu.make_async_copy(assign_ref, slot_ref, sem.at[LOADS])
    slots.start()
    step = width // LOADS
    loads = []
    for at in range(LOADS):
        low = max(at * step - HALF, 0)
        count = min((at + 1) * step - HALF, seg_len) - low
        target = pad_ref.at[pl.ds(HALF + low, count)]
        loads.append(pltpu.make_async_copy(rec_ref.at[pl.ds(low, count)], target, sem.at[at]))
        loads[-1].start()
    pad_ref[pl.ds(0, HALF), :] = jnp.zeros((HALF, chans), BF16)
    pad_ref[pl.ds(HALF + seg_len, tail), :] = jnp.zeros((tail, chans), BF16)
    slots.wait()
    source = lax.broadcasted_iota(jnp.int32, (chans, chans), 0)
    pick = jnp.where(source == slot_ref[...], 1.0, 0.0)
    pick_ref[...] = pick.astype(BF16)
    turn_ref[...] = pick.T
    near = pl.multiple_of(win_ref[0] * half, half)
    far = pl.multiple_of((1 - win_ref[0]) * half, half)
    count = near_ref.shape[0]
    rest = half - count
    rows_ref[pl.ds(0, rest), :] = turn_ref[pl.ds(near + count, rest), :].astype(BF16)
    rows_ref[pl.ds(rest, half), :] = turn_ref[pl.ds(far, half), :].astype(BF16)
    rows = turn_ref[pl.ds(near, count), :].astype(BF16)
    for at in range(LOADS):
        loads[at].wait()
        store_turned(rows, pad_ref, at * step, step, (near_ref,))


def rest_body(mask_ref, pad_ref, rows_ref, pick_ref, own_ref, meta_ref, *out_refs):
    width, chans = pad_ref.shape
    mask = mask_ref[0, 0].astype(F32)
    meta_ref[...] = jnp.full(meta_ref.shape, mask, F32)
    store_turned(rows_ref[...], pad_ref, 0, width, out_refs)
    for out_ref in out_refs:
        ending = out_ref[:, pl.ds(width - 128, 128)].astype(F32)
        last = lax.broadcasted_iota(jnp.int32, ending.shape, 1) == 127
        out_ref[:, pl.ds(width - 128, 128)] = jnp.where(last, mask, ending).astype(BF16)
    ordered = jnp.dot(pad_ref[...], pick_ref[...], preferred_element_type=F32)
    own_ref[pl.ds(0, width), :] = ordered.astype(BF16)
    own_ref[pl.ds(width, HALF), :] = jnp.zeros((HALF, chans), BF16)
    own_ref[pl.ds(width + HALF, 16), :] = jnp.full((16, chans), mask, F32).astype(BF16)


def correlate(part, own_ref, lhs_ref):
    count, width = part.shape
    pack = GROUP // count
    if pack == 2:
        part = jnp.concatenate([part, pltpu.roll(part, width - 1, 1)], axis=0)
    for lag in range(0, HALF, pack):
        moved = part if lag == 0 else pltpu.roll(part, width - lag, 1)
        lhs_ref[pl.ds(lag * count, GROUP), :] = moved
    rhs = jnp.concatenate([own_ref[pl.ds(HALF, width), :], own_ref[pl.ds(0, width), :]], axis=1)
    return jnp.dot(lhs_ref[...], rhs, preferred_element_type=F32)


def first_body(own_ref, part_ref, *refs):
    term_ref, lhs_ref = refs[-2:]

    def step(at, carry):
        part = part_ref[pl.ds(pl.multiple_of(at * GROUP, GROUP), GROUP), :]
        terms = correlate(part, own_ref, lhs_ref).astype(BF16)
        term_ref[pl.ds(pl.multiple_of(at * GROUP * HALF, GROUP), GROUP * HALF), :] = terms
        return carry

    lax.fori_loop(0, part_ref.shape[0] // GROUP, step, 0)


def second_body(before, row, skip, final, seg_len, meta_ref, own_ref, part_ref, mark_ref, term_ref, *refs):
    lhs_ref, sem = refs[-2:]
    count, width = part_ref.shape
    chans = own_ref.shape[1]
    outs = []
    if before:
        prior_ref = refs[0]
        out_ref = refs[2] if row > before else refs[1]
        target = out_ref.at[pl.ds((row - before) * LAGS, before * LAGS)]
        outs.append(pltpu.make_async_copy(prior_ref, target, sem.at[0]))
        outs[-1].start()
    done_ref = refs[-3]
    ending = pl.ds(width - 128, 128)
    here = meta_ref[pl.ds(0, count), :] * mark_ref[pl.ds(0, count), ending].astype(F32)
    there = own_ref[pl.ds(width + HALF, count), :].astype(F32) * part_ref[:, ending].astype(F32)
    here = here[:, 127:128]
    there = there[:, 127:128]
    scale = 1.0 / (jnp.maximum(here + there, 1.0) * math.sqrt(seg_len))
    here = jnp.broadcast_to(here * scale, (count, chans))
    there = jnp.broadcast_to(there * scale, (count, chans))
    terms = correlate(part_ref[...], own_ref, lhs_ref).astype(BF16).astype(F32)
    slab = 8
    for low in range(0, count, slab):
        at = skip + low
        held_at = at // GROUP * GROUP * HALF + at % GROUP
        for lag in range(HALF):
            for high in range(2):
                lanes = pl.ds(high * chans, chans)
                line = lag * count + low
                mine = terms[line : line + slab, high * chans : (high + 1) * chans]
                held = term_ref[pl.ds(held_at + lag * GROUP, slab), lanes].astype(F32)
                total = mine * there[low : low + slab] + held * here[low : low + slab]
                done_ref[pl.ds(low * LAGS + high * HALF + lag, slab, stride=LAGS), :] = total
        if final:
            source = done_ref.at[pl.ds(low * LAGS, slab * LAGS)]
            target = out_ref.at[pl.ds((row + low) * LAGS, slab * LAGS)]
            outs.append(pltpu.make_async_copy(source, target, sem.at[1 + low // slab]))
            outs[-1].start()
    for out in outs:
        out.wait()


def body(records, assign, plan, seg_mask):
    chans, seg_count, seg_len = records.shape
    blocks = lax.axis_size("chan")
    half = chans // lax.axis_size("win")
    width = -(-(seg_len + LAGS) // 256) * 256
    win = lax.axis_index("win").astype(jnp.int32).reshape(1)
    rec = records.reshape(chans, seg_count * seg_len).T
    slots = assign.reshape(1, chans)
    per_near = half // NEARS
    shape = jax.ShapeDtypeStruct
    near_prep = pl.pallas_call(
        near_body,
        out_shape=(
            shape((per_near, width), BF16),
            shape((width, chans), BF16),
            shape((2 * half - per_near, chans), BF16),
            shape((chans, chans), BF16),
        ),
        in_specs=[SMEM, HBM, HBM],
        out_specs=(VMEM,) * 4,
        scratch_shapes=[
            pltpu.VMEM((chans, chans), F32),
            pltpu.VMEM((1, chans), jnp.int32),
            pltpu.SemaphoreType.DMA((LOADS + 1,)),
        ],
        compiler_params=NEAR_PARAMS,
        cost_estimate=pl.CostEstimate(flops=1 << 26, bytes_accessed=1 << 20, transcendentals=0),
        name="near_prep",
    )
    counts = (per_near,) * (NEARS - 1) + FARS
    rest_prep = pl.pallas_call(
        rest_body,
        out_shape=(shape((width + HALF + 16, chans), BF16), shape((16, 128), F32))
        + tuple(shape((count, width), BF16) for count in counts),
        in_specs=[SMEM] + [VMEM] * 3,
        out_specs=(VMEM,) * (len(counts) + 2),
        compiler_params=PARAMS,
        cost_estimate=pl.CostEstimate(flops=1 << 27, bytes_accessed=1 << 20, transcendentals=0),
        name="rest_prep",
    )
    rows = GROUP * HALF
    flops = 2 * rows * width * 2 * chans
    lhs = pltpu.VMEM((rows, width), BF16)

    def first(*args):
        return pl.pallas_call(
            first_body,
            out_shape=shape((per_near * HALF, 2 * chans), BF16),
            in_specs=[VMEM, VMEM] + [ANY] * (len(args) - 2),
            out_specs=VMEM,
            scratch_shapes=[lhs],
            compiler_params=PARAMS,
            cost_estimate=pl.CostEstimate(flops=2 * flops, bytes_accessed=1 << 20, transcendentals=0),
            name="first",
        )(*args)

    def second(before, row, count):
        skip = row % per_near
        final = row + count == half
        total = shape((half * LAGS, chans), F32)
        done = shape((count * LAGS, chans), F32)
        lines = pltpu.VMEM((count * HALF, width), BF16)
        sems = pltpu.SemaphoreType.DMA((3,))
        if final:
            extra = dict(out_shape=(total,), out_specs=(ANY,))
            scratch = [pltpu.VMEM(done.shape, F32), lines, sems]
        elif before:
            extra = dict(out_shape=(total, done), out_specs=(ANY, VMEM))
            scratch = [lines, sems]
        else:
            extra = dict(out_shape=(done,), out_specs=(VMEM,))
            scratch = [lines, sems]
        return pl.pallas_call(
            lambda *refs: second_body(before, row, skip, final, seg_len, *refs),
            in_specs=[VMEM] * 5 + [VMEM] * (before > 0) + [ANY] * (row > before),
            scratch_shapes=scratch,
            input_output_aliases={6: 0} if row > before else {},
            compiler_params=PARAMS,
            cost_estimate=pl.CostEstimate(flops=flops, bytes_accessed=1 << 20, transcendentals=0),
            name="second",
            **extra,
        )

    def exchange(bit):
        straight = []
        crossed = []
        for low in range(blocks):
            for core in range(2):
                straight.append((low * 2 + core, (low ^ 1 << bit) * 2 + core))
                crossed.append((low * 2 + core, (low ^ 1 << bit) * 2 + 1 - core))

        def run(near0, pad, turned, pick, flags):
            own, meta, *pieces = rest_prep(flags, pad, turned, pick)
            near = []
            for one in [near0] + pieces[: NEARS - 1]:
                near.append(lax.ppermute(one, ("chan", "win"), straight))
            far = []
            for one in pieces[NEARS - 1 :]:
                far.append(lax.ppermute(one, ("chan", "win"), crossed))
            other = lax.ppermute(own, "win", [(0, 1), (1, 0)])
            terms = []
            for one in near:
                terms.append(first(own, one, *terms[-1:]))
            out = done = ()
            before = row = 0
            for one in far:
                count = one.shape[0]
                side = row // per_near
                step = second(before, row, count)
                result = step(meta, other, one, near[-1], terms[side], *done, *out)
                out = result[:1] if before else ()
                done = result[-1:]
                before = count
                row += count
            return out[0]

        return run

    digits = blocks.bit_length() - 1
    held = near_prep(win, rec, slots)
    branches = [exchange(bit) for bit in range(digits)]
    out = lax.switch(plan[0], branches, *held, seg_mask)
    return jnp.transpose(out.reshape(half, LAGS, chans), (2, 0, 1))[None]


def solution(mesh):
    placed = (P(("days", "chan"), "win", None), P("chan"), P(), P(("days", "chan"), "win"))
    return jax.shard_map(
        body, mesh=mesh, in_specs=placed, out_specs=P("days", "chan", "win", None), check_vma=False
    )
```

```python
import math

import jax
import jax.numpy as jnp
from jax import lax
from jax.experimental import pallas as pl
from jax.experimental.pallas import tpu as pltpu
from jax.sharding import PartitionSpec as P


LAGS = 64
HALF = LAGS // 2
GROUP = 16
NEARS = 2
LOADS = 1
FARS = (16, 16, 16, 16)
BF16 = jnp.bfloat16
F32 = jnp.float32
PARAMS = pltpu.CompilerParams(vmem_limit_bytes=24 * 1024 * 1024)

NEAR_PARAMS = pltpu.CompilerParams(vmem_limit_bytes=62 * 1024 * 1024)
SMEM = pl.BlockSpec(memory_space=pltpu.SMEM)
VMEM = pl.BlockSpec(memory_space=pltpu.VMEM)
ANY = pl.BlockSpec(memory_space=pl.ANY)
HBM = pl.BlockSpec(memory_space=pltpu.HBM)


def store_turned(rows, pad_ref, start, size, out_refs):
    turned = lax.dot_general(
        rows, pad_ref[pl.ds(start, size), :], (((1,), (1,)), ((), ())), preferred_element_type=F32
    )
    at = 0
    for out_ref in out_refs:
        count = out_ref.shape[0]
        out_ref[:, pl.ds(start, size)] = turned[at : at + count].astype(BF16)
        at += count


def near_body(win_ref, rec_ref, assign_ref, near_ref, pad_ref, rows_ref, pick_ref, turn_ref, slot_ref, sem):
    seg_len, chans = rec_ref.shape
    width = pad_ref.shape[0]
    half = chans // 2
    tail = width - HALF - seg_len
    slots = pltpu.make_async_copy(assign_ref, slot_ref, sem.at[LOADS])
    slots.start()
    step = width // LOADS
    loads = []
    for at in range(LOADS):
        low = max(at * step - HALF, 0)
        count = min((at + 1) * step - HALF, seg_len) - low
        target = pad_ref.at[pl.ds(HALF + low, count)]
        loads.append(pltpu.make_async_copy(rec_ref.at[pl.ds(low, count)], target, sem.at[at]))
        loads[-1].start()
    pad_ref[pl.ds(0, HALF), :] = jnp.zeros((HALF, chans), BF16)
    pad_ref[pl.ds(HALF + seg_len, tail), :] = jnp.zeros((tail, chans), BF16)
    slots.wait()
    source = lax.broadcasted_iota(jnp.int32, (chans, chans), 0)
    pick = jnp.where(source == slot_ref[...], 1.0, 0.0)
    pick_ref[...] = pick.astype(BF16)
    turn_ref[...] = pick.T
    near = pl.multiple_of(win_ref[0] * half, half)
    far = pl.multiple_of((1 - win_ref[0]) * half, half)
    count = near_ref.shape[0]
    rest = half - count
    rows_ref[pl.ds(0, rest), :] = turn_ref[pl.ds(near + count, rest), :].astype(BF16)
    rows_ref[pl.ds(rest, half), :] = turn_ref[pl.ds(far, half), :].astype(BF16)
    rows = turn_ref[pl.ds(near, count), :].astype(BF16)
    for at in range(LOADS):
        loads[at].wait()
        store_turned(rows, pad_ref, at * step, step, (near_ref,))


def rest_body(mask_ref, pad_ref, rows_ref, pick_ref, own_ref, meta_ref, *out_refs):
    width, chans = pad_ref.shape
    mask = mask_ref[0, 0].astype(F32)
    meta_ref[...] = jnp.full(meta_ref.shape, mask, F32)
    store_turned(rows_ref[...], pad_ref, 0, width, out_refs)
    for out_ref in out_refs:
        ending = out_ref[:, pl.ds(width - 128, 128)].astype(F32)
        last = lax.broadcasted_iota(jnp.int32, ending.shape, 1) == 127
        out_ref[:, pl.ds(width - 128, 128)] = jnp.where(last, mask, ending).astype(BF16)
    ordered = jnp.dot(pad_ref[...], pick_ref[...], preferred_element_type=F32)
    own_ref[pl.ds(0, width), :] = ordered.astype(BF16)
    own_ref[pl.ds(width, HALF), :] = jnp.zeros((HALF, chans), BF16)
    own_ref[pl.ds(width + HALF, 16), :] = jnp.full((16, chans), mask, F32).astype(BF16)


def correlate(part, own_ref, lhs_ref):
    count, width = part.shape
    pack = GROUP // count
    if pack == 2:
        part = jnp.concatenate([part, pltpu.roll(part, width - 1, 1)], axis=0)
    for lag in range(0, HALF, pack):
        moved = part if lag == 0 else pltpu.roll(part, width - lag, 1)
        lhs_ref[pl.ds(lag * count, GROUP), :] = moved
    rhs = jnp.concatenate([own_ref[pl.ds(HALF, width), :], own_ref[pl.ds(0, width), :]], axis=1)
    return jnp.dot(lhs_ref[...], rhs, preferred_element_type=F32)


def first_body(own_ref, part_ref, *refs):
    term_ref, lhs_ref = refs[-2:]

    def step(at, carry):
        part = part_ref[pl.ds(pl.multiple_of(at * GROUP, GROUP), GROUP), :]
        terms = correlate(part, own_ref, lhs_ref).astype(BF16)
        term_ref[pl.ds(pl.multiple_of(at * GROUP * HALF, GROUP), GROUP * HALF), :] = terms
        return carry

    lax.fori_loop(0, part_ref.shape[0] // GROUP, step, 0)


def second_body(before, row, skip, final, seg_len, meta_ref, own_ref, part_ref, mark_ref, term_ref, *refs):
    lhs_ref, sem, gate = refs[-3:]
    count, width = part_ref.shape
    chans = own_ref.shape[1]
    outs = []
    if before:
        prior_ref = refs[0]
        out_ref = refs[2] if row > before else refs[1]
        target = out_ref.at[pl.ds((row - before) * LAGS, before * LAGS)]
        outs.append(pltpu.make_async_copy(prior_ref, target, sem.at[0]))
        outs[-1].start()
        pl.semaphore_signal(gate, 1)
        pl.semaphore_wait(gate, 1)
    done_ref = refs[-4]
    ending = pl.ds(width - 128, 128)
    here = meta_ref[pl.ds(0, count), :] * mark_ref[pl.ds(0, count), ending].astype(F32)
    there = own_ref[pl.ds(width + HALF, count), :].astype(F32) * part_ref[:, ending].astype(F32)
    here = here[:, 127:128]
    there = there[:, 127:128]
    scale = 1.0 / (jnp.maximum(here + there, 1.0) * math.sqrt(seg_len))
    here = jnp.broadcast_to(here * scale, (count, chans))
    there = jnp.broadcast_to(there * scale, (count, chans))
    terms = correlate(part_ref[...], own_ref, lhs_ref).astype(BF16).astype(F32)
    slab = 8
    for low in range(0, count, slab):
        at = skip + low
        held_at = at // GROUP * GROUP * HALF + at % GROUP
        for high in range(2):
            lanes = pl.ds(high * chans, chans)
            for first in range(0, HALF, 8):
                tiles = []
                for lag in range(first, first + 8):
                    line = lag * count + low
                    mine = terms[line : line + slab, high * chans : (high + 1) * chans]
                    held = term_ref[pl.ds(held_at + lag * GROUP, slab), lanes].astype(F32)
                    tiles.append(mine * there[low : low + slab] + held * here[low : low + slab])
                turned = jnp.transpose(jnp.stack(tiles, 0), (1, 0, 2))
                for one in range(slab):
                    spot = (low + one) * LAGS + high * HALF + first
                    done_ref[pl.ds(spot, 8), :] = turned[one]
        if final:
            source = done_ref.at[pl.ds(low * LAGS, slab * LAGS)]
            target = out_ref.at[pl.ds((row + low) * LAGS, slab * LAGS)]
            outs.append(pltpu.make_async_copy(source, target, sem.at[1 + low // slab]))
            outs[-1].start()
    for out in outs:
        out.wait()


def body(records, assign, plan, seg_mask):
    chans, seg_count, seg_len = records.shape
    blocks = lax.axis_size("chan")
    half = chans // lax.axis_size("win")
    width = -(-(seg_len + LAGS) // 256) * 256
    win = lax.axis_index("win").astype(jnp.int32).reshape(1)
    rec = records.reshape(chans, seg_count * seg_len).T
    slots = assign.reshape(1, chans)
    per_near = half // NEARS
    shape = jax.ShapeDtypeStruct
    near_prep = pl.pallas_call(
        near_body,
        out_shape=(
            shape((per_near, width), BF16),
            shape((width, chans), BF16),
            shape((2 * half - per_near, chans), BF16),
            shape((chans, chans), BF16),
        ),
        in_specs=[SMEM, HBM, HBM],
        out_specs=(VMEM,) * 4,
        scratch_shapes=[
            pltpu.VMEM((chans, chans), F32),
            pltpu.VMEM((1, chans), jnp.int32),
            pltpu.SemaphoreType.DMA((LOADS + 1,)),
        ],
        compiler_params=NEAR_PARAMS,
        cost_estimate=pl.CostEstimate(flops=1 << 26, bytes_accessed=1 << 20, transcendentals=0),
        name="near_prep",
    )
    counts = (per_near,) * (NEARS - 1) + FARS
    rest_prep = pl.pallas_call(
        rest_body,
        out_shape=(shape((width + HALF + 16, chans), BF16), shape((16, 128), F32))
        + tuple(shape((count, width), BF16) for count in counts),
        in_specs=[SMEM] + [VMEM] * 3,
        out_specs=(VMEM,) * (len(counts) + 2),
        compiler_params=PARAMS,
        cost_estimate=pl.CostEstimate(flops=1 << 27, bytes_accessed=1 << 20, transcendentals=0),
        name="rest_prep",
    )
    rows = GROUP * HALF
    flops = 2 * rows * width * 2 * chans
    lhs = pltpu.VMEM((rows, width), BF16)

    def first(*args):
        return pl.pallas_call(
            first_body,
            out_shape=shape((per_near * HALF, 2 * chans), BF16),
            in_specs=[VMEM, VMEM] + [ANY] * (len(args) - 2),
            out_specs=VMEM,
            scratch_shapes=[lhs],
            compiler_params=PARAMS,
            cost_estimate=pl.CostEstimate(flops=2 * flops, bytes_accessed=1 << 20, transcendentals=0),
            name="first",
        )(*args)

    def second(before, row, count):
        skip = row % per_near
        final = row + count == half
        total = shape((half * LAGS, chans), F32)
        done = shape((count * LAGS, chans), F32)
        lines = pltpu.VMEM((count * HALF, width), BF16)
        sems = pltpu.SemaphoreType.DMA((3,))
        gate = pltpu.SemaphoreType.REGULAR
        if final:
            extra = dict(out_shape=(total,), out_specs=(ANY,))
            scratch = [pltpu.VMEM(done.shape, F32), lines, sems, gate]
        elif before:
            extra = dict(out_shape=(total, done), out_specs=(ANY, VMEM))
            scratch = [lines, sems, gate]
        else:
            extra = dict(out_shape=(done,), out_specs=(VMEM,))
            scratch = [lines, sems, gate]
        return pl.pallas_call(
            lambda *refs: second_body(before, row, skip, final, seg_len, *refs),
            in_specs=[VMEM] * 5 + [VMEM] * (before > 0) + [ANY] * (row > before),
            scratch_shapes=scratch,
            input_output_aliases={6: 0} if row > before else {},
            compiler_params=PARAMS,
            cost_estimate=pl.CostEstimate(flops=flops, bytes_accessed=1 << 20, transcendentals=0),
            name="second",
            **extra,
        )

    def exchange(bit):
        straight = []
        crossed = []
        for low in range(blocks):
            for core in range(2):
                straight.append((low * 2 + core, (low ^ 1 << bit) * 2 + core))
                crossed.append((low * 2 + core, (low ^ 1 << bit) * 2 + 1 - core))

        def run(near0, pad, turned, pick, flags):
            own, meta, *pieces = rest_prep(flags, pad, turned, pick)
            near = []
            for one in [near0] + pieces[: NEARS - 1]:
                near.append(lax.ppermute(one, ("chan", "win"), straight))
            far = []
            for one in pieces[NEARS - 1 :]:
                far.append(lax.ppermute(one, ("chan", "win"), crossed))
            other = lax.ppermute(own, "win", [(0, 1), (1, 0)])
            terms = []
            for one in near:
                terms.append(first(own, one, *terms[-1:]))
            out = done = ()
            before = row = 0
            for one in far:
                count = one.shape[0]
                side = row // per_near
                step = second(before, row, count)
                result = step(meta, other, one, near[-1], terms[side], *done, *out)
                out = result[:1] if before else ()
                done = result[-1:]
                before = count
                row += count
            return out[0]

        return run

    digits = blocks.bit_length() - 1
    held = near_prep(win, rec, slots)
    branches = [exchange(bit) for bit in range(digits)]
    out = lax.switch(plan[0], branches, *held, seg_mask)
    return jnp.transpose(out.reshape(half, LAGS, chans), (2, 0, 1))[None]


def solution(mesh):
    placed = (P(("days", "chan"), "win", None), P("chan"), P(), P(("days", "chan"), "win"))
    return jax.shard_map(
        body, mesh=mesh, in_specs=placed, out_specs=P("days", "chan", "win", None), check_vma=False
    )
```

```python
import math

import jax
import jax.numpy as jnp
from jax import lax
from jax.experimental import pallas as pl
from jax.experimental.pallas import tpu as pltpu
from jax.sharding import PartitionSpec as P


LAGS = 64
HALF = LAGS // 2
GROUP = 16
ORDER = (('near', 32), ('near', 32), ('far', 16), ('far', 16), ('far', 16), ('far', 16))
BF16 = jnp.bfloat16
F32 = jnp.float32
PARAMS = pltpu.CompilerParams(vmem_limit_bytes=24 * 1024 * 1024)

NEAR_PARAMS = pltpu.CompilerParams(vmem_limit_bytes=62 * 1024 * 1024)
SMEM = pl.BlockSpec(memory_space=pltpu.SMEM)
VMEM = pl.BlockSpec(memory_space=pltpu.VMEM)
ANY = pl.BlockSpec(memory_space=pl.ANY)
HBM = pl.BlockSpec(memory_space=pltpu.HBM)


def turn(rows, times_ref):
    return lax.dot_general(
        rows, times_ref[...], (((1,), (1,)), ((), ())), preferred_element_type=F32
    ).astype(BF16)


def near_body(win_ref, rec_ref, assign_ref, head_ref, pad_ref, rows_ref, pick_ref, turn_ref, slot_ref, sem):
    chans = rec_ref.shape[1]
    half = chans // 2
    count = pad_ref.shape[0] - HALF
    slots = pltpu.make_async_copy(assign_ref, slot_ref, sem.at[0])
    load = pltpu.make_async_copy(rec_ref.at[pl.ds(0, count)], pad_ref.at[pl.ds(HALF, count)], sem.at[1])
    slots.start()
    load.start()
    pad_ref[pl.ds(0, HALF), :] = jnp.zeros((HALF, chans), BF16)
    slots.wait()
    source = lax.broadcasted_iota(jnp.int32, (chans, chans), 0)
    pick = jnp.where(source == slot_ref[...], 1.0, 0.0)
    pick_ref[...] = pick.astype(BF16)
    turn_ref[...] = pick.T
    near = pl.multiple_of(win_ref[0] * half, half)
    far = pl.multiple_of((1 - win_ref[0]) * half, half)
    rows = turn_ref[pl.ds(near, half), :].astype(BF16)
    rows_ref[pl.ds(0, half), :] = rows
    rows_ref[pl.ds(half, half), :] = turn_ref[pl.ds(far, half), :].astype(BF16)
    load.wait()
    head_ref[...] = turn(rows, pad_ref)


def rest_body(nears, mask_ref, rec_ref, pad_ref, rows_ref, pick_ref, own_ref, meta_ref, *refs):
    out_refs = refs[:-2]
    tail_ref, sem = refs[-2:]
    seg_len, chans = rec_ref.shape
    head = pad_ref.shape[0]
    rest = tail_ref.shape[0]
    half = chans // 2
    count = seg_len + HALF - head
    load = pltpu.make_async_copy(
        rec_ref.at[pl.ds(head - HALF, count)], tail_ref.at[pl.ds(0, count)], sem.at[0]
    )
    load.start()
    tail_ref[pl.ds(count, rest - count), :] = jnp.zeros((rest - count, chans), BF16)
    mask = mask_ref[0, 0].astype(F32)
    meta_ref[...] = jnp.full(meta_ref.shape, mask, F32)
    early = turn(rows_ref[pl.ds(half, half), :], pad_ref)
    at = 0
    for out_ref in out_refs[nears:]:
        out_ref[:, pl.ds(0, head)] = early[at : at + out_ref.shape[0]]
        at += out_ref.shape[0]
    own_ref[pl.ds(0, head), :] = jnp.dot(
        pad_ref[...], pick_ref[...], preferred_element_type=F32
    ).astype(BF16)
    own_ref[pl.ds(head + rest, HALF), :] = jnp.zeros((HALF, chans), BF16)
    own_ref[pl.ds(head + rest + HALF, 16), :] = jnp.full((16, chans), mask, F32).astype(BF16)
    load.wait()
    late = turn(rows_ref[...], tail_ref)
    last = lax.broadcasted_iota(jnp.int32, (chans, 128), 1) == 127
    ending = jnp.where(last, mask, late[:, rest - 128 :].astype(F32)).astype(BF16)
    at = 0
    for out_ref in out_refs:
        count, width = out_ref.shape
        out_ref[:, pl.ds(width - rest, rest - 128)] = late[at : at + count, : rest - 128]
        out_ref[:, pl.ds(width - 128, 128)] = ending[at : at + count]
        at += count
    own_ref[pl.ds(head, rest), :] = jnp.dot(
        tail_ref[...], pick_ref[...], preferred_element_type=F32
    ).astype(BF16)


def correlate(part, own_ref, lhs_ref):
    count, width = part.shape
    pack = GROUP // count
    if pack == 2:
        part = jnp.concatenate([part, pltpu.roll(part, width - 1, 1)], axis=0)
    for lag in range(0, HALF, pack):
        moved = part if lag == 0 else pltpu.roll(part, width - lag, 1)
        lhs_ref[pl.ds(lag * count, GROUP), :] = moved
    rhs = jnp.concatenate([own_ref[pl.ds(HALF, width), :], own_ref[pl.ds(0, width), :]], axis=1)
    return jnp.dot(lhs_ref[...], rhs, preferred_element_type=F32)


def first_body(row, own_ref, head_ref, part_ref, *refs):
    term_ref, lhs_ref = refs[-2:]

    def step(at, carry):
        early = head_ref[pl.ds(pl.multiple_of(row + at * GROUP, GROUP), GROUP), :]
        late = part_ref[pl.ds(pl.multiple_of(at * GROUP, GROUP), GROUP), :]
        terms = correlate(jnp.concatenate([early, late], axis=1), own_ref, lhs_ref).astype(BF16)
        term_ref[pl.ds(pl.multiple_of(at * GROUP * HALF, GROUP), GROUP * HALF), :] = terms
        return carry

    lax.fori_loop(0, part_ref.shape[0] // GROUP, step, 0)


def second_body(given, before, row, skip, final, seg_len, meta_ref, own_ref, part_ref, mark_ref, term_ref, *refs):
    lhs_ref, sem, gate = refs[-3:]
    count, width = part_ref.shape
    chans = own_ref.shape[1]
    outs = []
    if before:
        prior_ref = refs[0]
        out_ref = refs[given]
        target = out_ref.at[pl.ds((row - before) * LAGS, before * LAGS)]
        outs.append(pltpu.make_async_copy(prior_ref, target, sem.at[0]))
        outs[-1].start()
        pl.semaphore_signal(gate, 1)
        pl.semaphore_wait(gate, 1)
    done_ref = refs[-4]
    ending = pl.ds(width - 128, 128)
    here = meta_ref[pl.ds(0, count), :] * mark_ref[pl.ds(0, count), pl.ds(mark_ref.shape[1] - 128, 128)].astype(F32)
    there = own_ref[pl.ds(width + HALF, count), :].astype(F32) * part_ref[:, ending].astype(F32)
    here = here[:, 127:128]
    there = there[:, 127:128]
    scale = 1.0 / (jnp.maximum(here + there, 1.0) * math.sqrt(seg_len))
    here = jnp.broadcast_to(here * scale, (count, chans))
    there = jnp.broadcast_to(there * scale, (count, chans))
    terms = correlate(part_ref[...], own_ref, lhs_ref).astype(BF16).astype(F32)
    slab = 8
    for low in range(0, count, slab):
        at = skip + low
        held_at = at // GROUP * GROUP * HALF + at % GROUP
        for high in range(2):
            lanes = pl.ds(high * chans, chans)
            for first in range(0, HALF, 8):
                tiles = []
                for lag in range(first, first + 8):
                    line = lag * count + low
                    mine = terms[line : line + slab, high * chans : (high + 1) * chans]
                    held = term_ref[pl.ds(held_at + lag * GROUP, slab), lanes].astype(F32)
                    tiles.append(mine * there[low : low + slab] + held * here[low : low + slab])
                turned = jnp.transpose(jnp.stack(tiles, 0), (1, 0, 2))
                for one in range(slab):
                    spot = (low + one) * LAGS + high * HALF + first
                    done_ref[pl.ds(spot, 8), :] = turned[one]
        if final:
            source = done_ref.at[pl.ds(low * LAGS, slab * LAGS)]
            target = out_ref.at[pl.ds((row + low) * LAGS, slab * LAGS)]
            outs.append(pltpu.make_async_copy(source, target, sem.at[1 + low // slab]))
            outs[-1].start()
    for out in outs:
        out.wait()


def body(records, assign, plan, seg_mask):
    chans, seg_count, seg_len = records.shape
    blocks = lax.axis_size("chan")
    half = chans // lax.axis_size("win")
    width = -(-(seg_len + LAGS) // 256) * 256
    win = lax.axis_index("win").astype(jnp.int32).reshape(1)
    rec = records.reshape(chans, seg_count * seg_len).T
    slots = assign.reshape(1, chans)
    nears = [count for side, count in ORDER if side == "near"]
    fars = [count for side, count in ORDER if side == "far"]
    shape = jax.ShapeDtypeStruct
    head = width // 256 * 128
    near_prep = pl.pallas_call(
        near_body,
        out_shape=(
            shape((half, head), BF16),
            shape((head, chans), BF16),
            shape((chans, chans), BF16),
            shape((chans, chans), BF16),
        ),
        in_specs=[SMEM, HBM, HBM],
        out_specs=(VMEM,) * 4,
        scratch_shapes=[
            pltpu.VMEM((chans, chans), F32),
            pltpu.VMEM((1, chans), jnp.int32),
            pltpu.SemaphoreType.DMA((2,)),
        ],
        compiler_params=NEAR_PARAMS,
        cost_estimate=pl.CostEstimate(flops=1 << 26, bytes_accessed=1 << 20, transcendentals=0),
        name="near_prep",
    )
    rest_prep = pl.pallas_call(
        lambda *refs: rest_body(len(nears), *refs),
        out_shape=(shape((width + HALF + 16, chans), BF16), shape((16, 128), F32))
        + tuple(shape((count, width - head), BF16) for count in nears)
        + tuple(shape((count, width), BF16) for count in fars),
        in_specs=[SMEM, HBM] + [VMEM] * 3,
        out_specs=(VMEM,) * (len(ORDER) + 2),
        scratch_shapes=[pltpu.VMEM((width - head, chans), BF16), pltpu.SemaphoreType.DMA((1,))],
        compiler_params=PARAMS,
        cost_estimate=pl.CostEstimate(flops=1 << 27, bytes_accessed=1 << 20, transcendentals=0),
        name="rest_prep",
    )
    rows = GROUP * HALF
    flops = 2 * rows * width * 2 * chans
    lhs = pltpu.VMEM((rows, width), BF16)

    def first(row, *args):
        count = args[2].shape[0]
        return pl.pallas_call(
            lambda *refs: first_body(row, *refs),
            out_shape=shape((count * HALF, 2 * chans), BF16),
            in_specs=[VMEM] * 3 + [ANY] * (len(args) - 3),
            out_specs=VMEM,
            scratch_shapes=[lhs],
            compiler_params=PARAMS,
            cost_estimate=pl.CostEstimate(
                flops=flops * count // GROUP, bytes_accessed=1 << 20, transcendentals=0
            ),
            name="first",
        )(*args)

    def second(before, row, skip, meta, other, part, mark, terms, done, out, after):
        count = part.shape[0]
        final = row + count == half
        total = shape((half * LAGS, chans), F32)
        held = shape((count * LAGS, chans), F32)
        scratch = [
            pltpu.VMEM((count * HALF, width), BF16),
            pltpu.SemaphoreType.DMA((3,)),
            pltpu.SemaphoreType.REGULAR,
        ]
        if final:
            extra = dict(out_shape=(total,), out_specs=(ANY,))
            scratch = [pltpu.VMEM(held.shape, F32)] + scratch
        elif before:
            extra = dict(out_shape=(total, held), out_specs=(ANY, VMEM))
        else:
            extra = dict(out_shape=(held,), out_specs=(VMEM,))
        given = len(done) + len(out) + len(after)
        return pl.pallas_call(
            lambda *refs: second_body(given, before, row, skip, final, seg_len, *refs),
            in_specs=[VMEM] * (5 + len(done)) + [ANY] * (len(out) + len(after)),
            scratch_shapes=scratch,
            input_output_aliases={6: 0} if out else {},
            compiler_params=PARAMS,
            cost_estimate=pl.CostEstimate(
                flops=flops * count // GROUP, bytes_accessed=1 << 20, transcendentals=0
            ),
            name="second",
            **extra,
        )(meta, other, part, mark, terms, *done, *out, *after)

    def exchange(bit):
        straight = []
        crossed = []
        for low in range(blocks):
            for core in range(2):
                straight.append((low * 2 + core, (low ^ 1 << bit) * 2 + core))
                crossed.append((low * 2 + core, (low ^ 1 << bit) * 2 + 1 - core))

        def run(head, pad, turned, pick, rec, flags):
            own, meta, *pieces = rest_prep(flags, rec, pad, turned, pick)
            opening = lax.ppermute(head, ("chan", "win"), straight)
            sent = {"near": pieces[: len(nears)], "far": pieces[len(nears) :]}
            routes = {"near": straight, "far": crossed}
            came = {"near": [], "far": []}
            for at, (side, _) in enumerate(ORDER):
                one = sent[side][len(came[side])]
                came[side].append(lax.ppermute(one, ("chan", "win"), routes[side]))
            other = lax.ppermute(own, "win", [(0, 1), (1, 0)])
            terms = []
            starts = [sum(nears[:at]) for at in range(len(nears))]
            done = out = after = ()
            before = row = taken = 0
            for side, count in ORDER:
                if side == "near":
                    at = len(terms)
                    terms.append(first(starts[at], own, opening, came["near"][at], *after, *done[:1]))
                    after = (terms[-1],)
                    continue
                home = max(at for at in range(len(nears)) if starts[at] <= row)
                after = after[: after != () and after[0] is not terms[home]]
                part = came["far"][taken]
                skip = row - starts[home]
                result = second(before, row, skip, meta, other, part, came["near"][0], terms[home], done, out, after)
                out = result[:1] if before else ()
                done = result[-1:]
                after = ()
                before = count
                row += count
                taken += 1
            return out[0]

        return run

    digits = blocks.bit_length() - 1
    held = near_prep(win, rec, slots)
    branches = [exchange(bit) for bit in range(digits)]
    out = lax.switch(plan[0], branches, *held, rec, seg_mask)
    return jnp.transpose(out.reshape(half, LAGS, chans), (2, 0, 1))[None]


def solution(mesh):
    placed = (P(("days", "chan"), "win", None), P("chan"), P(), P(("days", "chan"), "win"))
    return jax.shard_map(
        body, mesh=mesh, in_specs=placed, out_specs=P("days", "chan", "win", None), check_vma=False
    )
```

```python
import math

import jax
import jax.numpy as jnp
from jax import lax
from jax.experimental import pallas as pl
from jax.experimental.pallas import tpu as pltpu
from jax.sharding import PartitionSpec as P


LAGS = 64
HALF = LAGS // 2
GROUP = 16
TILE = 128
ORDER = (('near', 32), ('near', 32), ('far', 16), ('far', 16), ('far', 16), ('far', 16))
BF16 = jnp.bfloat16
F32 = jnp.float32
PARAMS = pltpu.CompilerParams(vmem_limit_bytes=24 * 1024 * 1024)

NEAR_PARAMS = pltpu.CompilerParams(vmem_limit_bytes=62 * 1024 * 1024)
SMEM = pl.BlockSpec(memory_space=pltpu.SMEM)
VMEM = pl.BlockSpec(memory_space=pltpu.VMEM)
ANY = pl.BlockSpec(memory_space=pl.ANY)
HBM = pl.BlockSpec(memory_space=pltpu.HBM)


def turn(rows, times_ref):
    return lax.dot_general(
        rows, times_ref[...], (((1,), (1,)), ((), ())), preferred_element_type=F32
    ).astype(BF16)


def near_body(win_ref, rec_ref, assign_ref, head_ref, times_ref, rows_ref, pick_ref, turn_ref, slot_ref, sem):
    chans = rec_ref.shape[1]
    half = chans // 2
    slots = pltpu.make_async_copy(assign_ref, slot_ref, sem.at[0])
    load = pltpu.make_async_copy(rec_ref.at[pl.ds(0, times_ref.shape[0])], times_ref, sem.at[1])
    slots.start()
    load.start()
    slots.wait()
    source = lax.broadcasted_iota(jnp.int32, (chans, chans), 0)
    pick = jnp.where(source == slot_ref[...], 1.0, 0.0)
    pick_ref[...] = pick.astype(BF16)
    turn_ref[...] = pick.T
    near = pl.multiple_of(win_ref[0] * half, half)
    far = pl.multiple_of((1 - win_ref[0]) * half, half)
    rows = turn_ref[pl.ds(near, half), :].astype(BF16)
    rows_ref[pl.ds(0, half), :] = rows
    rows_ref[pl.ds(half, half), :] = turn_ref[pl.ds(far, half), :].astype(BF16)
    load.wait()
    head_ref[...] = turn(rows, times_ref)


def rest_body(nears, mask_ref, rec_ref, times_ref, rows_ref, pick_ref, own_ref, meta_ref, *refs):
    out_refs = refs[:-2]
    tail_ref, sem = refs[-2:]
    seg_len, chans = rec_ref.shape
    head = times_ref.shape[0]
    rest = tail_ref.shape[0]
    half = chans // 2
    count = seg_len - head
    load = pltpu.make_async_copy(
        rec_ref.at[pl.ds(head, count)], tail_ref.at[pl.ds(0, count)], sem.at[0]
    )
    load.start()
    tail_ref[pl.ds(count, rest - count), :] = jnp.zeros((rest - count, chans), BF16)
    mask = mask_ref[0, 0].astype(F32)
    meta_ref[...] = jnp.full(meta_ref.shape, mask, F32)
    early = turn(rows_ref[pl.ds(half, half), :], times_ref)
    at = 0
    for out_ref in out_refs[nears:]:
        out_ref[:, pl.ds(0, head)] = early[at : at + out_ref.shape[0]]
        at += out_ref.shape[0]
    own_ref[pl.ds(0, HALF), :] = jnp.zeros((HALF, chans), BF16)
    own_ref[pl.ds(HALF, head), :] = jnp.dot(
        times_ref[...], pick_ref[...], preferred_element_type=F32
    ).astype(BF16)
    own_ref[pl.ds(HALF + head + rest, 16), :] = jnp.full((16, chans), mask, F32).astype(BF16)
    load.wait()
    late = turn(rows_ref[...], tail_ref)
    whole = rest - TILE
    at = 0
    for out_ref in out_refs:
        count, width = out_ref.shape
        host = width % (2 * TILE) == 0
        start = width - rest if host else width - whole
        out_ref[:, pl.ds(start, whole)] = late[at : at + count, :whole]
        if host:
            lane = lax.broadcasted_iota(jnp.int32, (count, TILE), 1)
            mine = late[at : at + count, whole:].astype(F32)
            guest = pltpu.roll(late[at + count : at + 2 * count, whole:].astype(F32), TILE // 2, 1)
            ending = jnp.where(lane == TILE - 1, mask, jnp.where(lane < TILE // 2, mine, guest))
            out_ref[:, pl.ds(width - TILE, TILE)] = ending.astype(BF16)
        at += count
    own_ref[pl.ds(HALF + head, rest), :] = jnp.dot(
        tail_ref[...], pick_ref[...], preferred_element_type=F32
    ).astype(BF16)


def ending(tile, guest, left):
    tile = tile.astype(F32)
    if guest:
        tile = pltpu.roll(tile, TILE // 2, 1)
    lane = lax.broadcasted_iota(jnp.int32, tile.shape, 1)
    return jnp.where(lane < left, tile, 0.0).astype(BF16)


def correlate(part, own_ref, lhs_ref):
    count, width = part.shape
    for lag in range(HALF):
        lhs_ref[pl.ds(lag * count, count), :] = pltpu.roll(part, HALF - lag, 1)
    rhs = jnp.concatenate([own_ref[pl.ds(HALF, width), :], own_ref[pl.ds(0, width), :]], axis=1)
    return jnp.dot(lhs_ref[...], rhs, preferred_element_type=F32)


def first_body(row, guest, left, own_ref, head_ref, part_ref, host_ref, *refs):
    term_ref, lhs_ref = refs[-2:]
    whole = host_ref.shape[1] - TILE

    def step(at, carry):
        rows = pl.ds(pl.multiple_of(at * GROUP, GROUP), GROUP)
        early = head_ref[pl.ds(pl.multiple_of(row + at * GROUP, GROUP), GROUP), :]
        last = ending(host_ref[rows, pl.ds(whole, TILE)], guest, left)
        part = jnp.concatenate([early, part_ref[rows, pl.ds(0, whole)], last], axis=1)
        terms = correlate(part, own_ref, lhs_ref).astype(BF16)
        term_ref[pl.ds(pl.multiple_of(at * GROUP * HALF, GROUP), GROUP * HALF), :] = terms
        return carry

    lax.fori_loop(0, part_ref.shape[0] // GROUP, step, 0)


def second_body(
    given, before, row, skip, guest, final, seg_len, meta_ref, own_ref, part_ref, host_ref, mark_ref, term_ref, *refs
):
    lhs_ref, sem, gate = refs[-3:]
    count, width = host_ref.shape
    chans = own_ref.shape[1]
    outs = []
    if before:
        prior_ref = refs[0]
        out_ref = refs[given]
        target = out_ref.at[pl.ds((row - before) * LAGS, before * LAGS)]
        outs.append(pltpu.make_async_copy(prior_ref, target, sem.at[0]))
        outs[-1].start()
        pl.semaphore_signal(gate, 1)
        pl.semaphore_wait(gate, 1)
    done_ref = refs[-4]
    tile = host_ref[:, pl.ds(width - TILE, TILE)]
    here = meta_ref[pl.ds(0, count), :] * mark_ref[pl.ds(0, count), pl.ds(mark_ref.shape[1] - TILE, TILE)].astype(F32)
    there = own_ref[pl.ds(width + HALF, count), :].astype(F32) * tile.astype(F32)
    here = here[:, TILE - 1 :]
    there = there[:, TILE - 1 :]
    scale = 1.0 / (jnp.maximum(here + there, 1.0) * math.sqrt(seg_len))
    here = jnp.broadcast_to(here * scale, (count, chans))
    there = jnp.broadcast_to(there * scale, (count, chans))
    last = ending(tile, guest, seg_len % TILE)
    part = jnp.concatenate([part_ref[:, pl.ds(0, width - TILE)], last], axis=1)
    terms = correlate(part, own_ref, lhs_ref).astype(BF16).astype(F32)
    slab = 8
    for low in range(0, count, slab):
        at = skip + low
        held_at = at // GROUP * GROUP * HALF + at % GROUP
        for high in range(2):
            lanes = pl.ds(high * chans, chans)
            for first in range(0, HALF, 8):
                tiles = []
                for lag in range(first, first + 8):
                    line = lag * count + low
                    mine = terms[line : line + slab, high * chans : (high + 1) * chans]
                    held = term_ref[pl.ds(held_at + lag * GROUP, slab), lanes].astype(F32)
                    tiles.append(mine * there[low : low + slab] + held * here[low : low + slab])
                turned = jnp.transpose(jnp.stack(tiles, 0), (1, 0, 2))
                for one in range(slab):
                    spot = (low + one) * LAGS + high * HALF + first
                    done_ref[pl.ds(spot, 8), :] = turned[one]
        if final:
            source = done_ref.at[pl.ds(low * LAGS, slab * LAGS)]
            target = out_ref.at[pl.ds((row + low) * LAGS, slab * LAGS)]
            outs.append(pltpu.make_async_copy(source, target, sem.at[1 + low // slab]))
            outs[-1].start()
    for out in outs:
        out.wait()


def body(records, assign, plan, seg_mask):
    chans, seg_count, seg_len = records.shape
    blocks = lax.axis_size("chan")
    half = chans // lax.axis_size("win")
    width = -(-(seg_len + LAGS) // (2 * TILE)) * 2 * TILE
    if width - TILE != seg_len // TILE * TILE or seg_len % TILE > TILE // 2:
        raise ValueError("segment length")
    win = lax.axis_index("win").astype(jnp.int32).reshape(1)
    rec = records.reshape(chans, seg_count * seg_len).T
    slots = assign.reshape(1, chans)
    nears = [count for side, count in ORDER if side == "near"]
    fars = [count for side, count in ORDER if side == "far"]
    shape = jax.ShapeDtypeStruct
    head = width // (4 * TILE) * 2 * TILE
    near_prep = pl.pallas_call(
        near_body,
        out_shape=(
            shape((half, head), BF16),
            shape((head, chans), BF16),
            shape((chans, chans), BF16),
            shape((chans, chans), BF16),
        ),
        in_specs=[SMEM, HBM, HBM],
        out_specs=(VMEM,) * 4,
        scratch_shapes=[
            pltpu.VMEM((chans, chans), F32),
            pltpu.VMEM((1, chans), jnp.int32),
            pltpu.SemaphoreType.DMA((2,)),
        ],
        compiler_params=NEAR_PARAMS,
        cost_estimate=pl.CostEstimate(flops=1 << 26, bytes_accessed=1 << 20, transcendentals=0),
        name="near_prep",
    )
    rest_prep = pl.pallas_call(
        lambda *refs: rest_body(len(nears), *refs),
        out_shape=(shape((width + HALF + 16, chans), BF16), shape((16, 128), F32))
        + tuple(shape((count, width - head - at % 2 * TILE), BF16) for at, count in enumerate(nears))
        + tuple(shape((count, width - at % 2 * TILE), BF16) for at, count in enumerate(fars)),
        in_specs=[SMEM, HBM] + [VMEM] * 3,
        out_specs=(VMEM,) * (len(ORDER) + 2),
        scratch_shapes=[pltpu.VMEM((width - head, chans), BF16), pltpu.SemaphoreType.DMA((1,))],
        compiler_params=PARAMS,
        cost_estimate=pl.CostEstimate(flops=1 << 27, bytes_accessed=1 << 20, transcendentals=0),
        name="rest_prep",
    )
    rows = GROUP * HALF
    flops = 2 * rows * width * 2 * chans
    lhs = pltpu.VMEM((rows, width), BF16)

    def first(row, guest, *args):
        count = args[2].shape[0]
        return pl.pallas_call(
            lambda *refs: first_body(row, guest, seg_len % TILE, *refs),
            out_shape=shape((count * HALF, 2 * chans), BF16),
            in_specs=[VMEM] * 4 + [ANY] * (len(args) - 4),
            out_specs=VMEM,
            scratch_shapes=[lhs],
            compiler_params=PARAMS,
            cost_estimate=pl.CostEstimate(
                flops=flops * count // GROUP, bytes_accessed=1 << 20, transcendentals=0
            ),
            name="first",
        )(*args)

    def second(before, row, skip, guest, meta, other, part, host, mark, terms, done, out, after):
        count = part.shape[0]
        final = row + count == half
        total = shape((half * LAGS, chans), F32)
        held = shape((count * LAGS, chans), F32)
        scratch = [
            pltpu.VMEM((count * HALF, width), BF16),
            pltpu.SemaphoreType.DMA((3,)),
            pltpu.SemaphoreType.REGULAR,
        ]
        if final:
            extra = dict(out_shape=(total,), out_specs=(ANY,))
            scratch = [pltpu.VMEM(held.shape, F32)] + scratch
        elif before:
            extra = dict(out_shape=(total, held), out_specs=(ANY, VMEM))
        else:
            extra = dict(out_shape=(held,), out_specs=(VMEM,))
        given = len(done) + len(out) + len(after)
        return pl.pallas_call(
            lambda *refs: second_body(given, before, row, skip, guest, final, seg_len, *refs),
            in_specs=[VMEM] * (6 + len(done)) + [ANY] * (len(out) + len(after)),
            scratch_shapes=scratch,
            input_output_aliases={7: 0} if out else {},
            compiler_params=PARAMS,
            cost_estimate=pl.CostEstimate(
                flops=flops * count // GROUP, bytes_accessed=1 << 20, transcendentals=0
            ),
            name="second",
            **extra,
        )(meta, other, part, host, mark, terms, *done, *out, *after)

    def exchange(bit):
        straight = []
        crossed = []
        for low in range(blocks):
            for core in range(2):
                straight.append((low * 2 + core, (low ^ 1 << bit) * 2 + core))
                crossed.append((low * 2 + core, (low ^ 1 << bit) * 2 + 1 - core))

        def run(head, pad, turned, pick, rec, flags):
            own, meta, *pieces = rest_prep(flags, rec, pad, turned, pick)
            opening = lax.ppermute(head, ("chan", "win"), straight)
            sent = {"near": pieces[: len(nears)], "far": pieces[len(nears) :]}
            routes = {"near": straight, "far": crossed}
            came = {"near": [], "far": []}
            for at, (side, _) in enumerate(ORDER):
                one = sent[side][len(came[side])]
                came[side].append(lax.ppermute(one, ("chan", "win"), routes[side]))
            other = lax.ppermute(own, "win", [(0, 1), (1, 0)])
            terms = []
            starts = [sum(nears[:at]) for at in range(len(nears))]
            done = out = after = ()
            before = row = taken = 0
            for side, count in ORDER:
                if side == "near":
                    at = len(terms)
                    guest = at % 2
                    parts = (came["near"][at], came["near"][at - guest])
                    terms.append(first(starts[at], guest, own, opening, *parts, *after, *done[:1]))
                    after = (terms[-1],)
                    continue
                home = max(at for at in range(len(nears)) if starts[at] <= row)
                after = after[: after != () and after[0] is not terms[home]]
                guest = taken % 2
                parts = (came["far"][taken], came["far"][taken - guest])
                skip = row - starts[home]
                result = second(
                    before, row, skip, guest, meta, other, *parts, came["near"][0], terms[home], done, out, after
                )
                out = result[:1] if before else ()
                done = result[-1:]
                after = ()
                before = count
                row += count
                taken += 1
            return out[0]

        return run

    digits = blocks.bit_length() - 1
    held = near_prep(win, rec, slots)
    branches = [exchange(bit) for bit in range(digits)]
    out = lax.switch(plan[0], branches, *held, rec, seg_mask)
    return jnp.transpose(out.reshape(half, LAGS, chans), (2, 0, 1))[None]


def solution(mesh):
    placed = (P(("days", "chan"), "win", None), P("chan"), P(), P(("days", "chan"), "win"))
    return jax.shard_map(
        body, mesh=mesh, in_specs=placed, out_specs=P("days", "chan", "win", None), check_vma=False
    )
```

```python
import math

import jax
import jax.numpy as jnp
from jax import lax
from jax.experimental import pallas as pl
from jax.experimental.pallas import tpu as pltpu
from jax.sharding import PartitionSpec as P


LAGS = 64
HALF = LAGS // 2
GROUP = 16
TILE = 128
ORDER = (('near', 32), ('near', 32), ('far', 16), ('far', 16), ('far', 16), ('far', 16))
BF16 = jnp.bfloat16
F32 = jnp.float32
PARAMS = pltpu.CompilerParams(vmem_limit_bytes=24 * 1024 * 1024)

NEAR_PARAMS = pltpu.CompilerParams(vmem_limit_bytes=62 * 1024 * 1024)
SMEM = pl.BlockSpec(memory_space=pltpu.SMEM)
VMEM = pl.BlockSpec(memory_space=pltpu.VMEM)
ANY = pl.BlockSpec(memory_space=pl.ANY)
HBM = pl.BlockSpec(memory_space=pltpu.HBM)


def turn(rows, times_ref):
    return lax.dot_general(
        rows, times_ref[...], (((1,), (1,)), ((), ())), preferred_element_type=F32
    ).astype(BF16)


def near_body(win_ref, rec_ref, assign_ref, head_ref, times_ref, rows_ref, pick_ref, turn_ref, slot_ref, sem):
    chans = rec_ref.shape[1]
    half = chans // 2
    slots = pltpu.make_async_copy(assign_ref, slot_ref, sem.at[0])
    load = pltpu.make_async_copy(rec_ref.at[pl.ds(0, times_ref.shape[0])], times_ref, sem.at[1])
    slots.start()
    load.start()
    slots.wait()
    source = lax.broadcasted_iota(jnp.int32, (chans, chans), 0)
    pick = jnp.where(source == slot_ref[...], 1.0, 0.0)
    pick_ref[...] = pick.astype(BF16)
    turn_ref[...] = pick.T
    near = pl.multiple_of(win_ref[0] * half, half)
    far = pl.multiple_of((1 - win_ref[0]) * half, half)
    rows = turn_ref[pl.ds(near, half), :].astype(BF16)
    rows_ref[pl.ds(0, half), :] = rows
    rows_ref[pl.ds(half, half), :] = turn_ref[pl.ds(far, half), :].astype(BF16)
    load.wait()
    head_ref[...] = turn(rows, times_ref)


def rest_body(nears, mask_ref, rec_ref, times_ref, rows_ref, pick_ref, own_ref, meta_ref, *refs):
    out_refs = refs[:-3]
    tail_ref, sem, gate = refs[-3:]
    seg_len, chans = rec_ref.shape
    head = times_ref.shape[0]
    rest = tail_ref.shape[0]
    half = chans // 2
    count = seg_len - head
    load = pltpu.make_async_copy(
        rec_ref.at[pl.ds(head, count)], tail_ref.at[pl.ds(0, count)], sem.at[0]
    )
    load.start()
    pl.semaphore_signal(gate, 1)
    pl.semaphore_wait(gate, 1)
    tail_ref[pl.ds(count, rest - count), :] = jnp.zeros((rest - count, chans), BF16)
    mask = mask_ref[0, 0].astype(F32)
    meta_ref[...] = jnp.full(meta_ref.shape, mask, F32)
    early = turn(rows_ref[pl.ds(half, half), :], times_ref)
    at = 0
    for out_ref in out_refs[nears:]:
        out_ref[:, pl.ds(0, head)] = early[at : at + out_ref.shape[0]]
        at += out_ref.shape[0]
    own_ref[pl.ds(0, HALF), :] = jnp.zeros((HALF, chans), BF16)
    own_ref[pl.ds(HALF, head), :] = jnp.dot(
        times_ref[...], pick_ref[...], preferred_element_type=F32
    ).astype(BF16)
    own_ref[pl.ds(HALF + head + rest, 16), :] = jnp.full((16, chans), mask, F32).astype(BF16)
    load.wait()
    late = turn(rows_ref[...], tail_ref)
    whole = rest - TILE
    at = 0
    for out_ref in out_refs:
        count, width = out_ref.shape
        host = width % (2 * TILE) == 0
        start = width - rest if host else width - whole
        out_ref[:, pl.ds(start, whole)] = late[at : at + count, :whole]
        if host:
            lane = lax.broadcasted_iota(jnp.int32, (count, TILE), 1)
            mine = late[at : at + count, whole:].astype(F32)
            guest = pltpu.roll(late[at + count : at + 2 * count, whole:].astype(F32), TILE // 2, 1)
            ending = jnp.where(lane == TILE - 1, mask, jnp.where(lane < TILE // 2, mine, guest))
            out_ref[:, pl.ds(width - TILE, TILE)] = ending.astype(BF16)
        at += count
    own_ref[pl.ds(HALF + head, rest), :] = jnp.dot(
        tail_ref[...], pick_ref[...], preferred_element_type=F32
    ).astype(BF16)


def ending(tile, guest, left):
    tile = tile.astype(F32)
    if guest:
        tile = pltpu.roll(tile, TILE // 2, 1)
    lane = lax.broadcasted_iota(jnp.int32, tile.shape, 1)
    return jnp.where(lane < left, tile, 0.0).astype(BF16)


def correlate(part, own_ref, lhs_ref):
    count, width = part.shape
    for lag in range(HALF):
        lhs_ref[pl.ds(lag * count, count), :] = pltpu.roll(part, HALF - lag, 1)
    rhs = jnp.concatenate([own_ref[pl.ds(HALF, width), :], own_ref[pl.ds(0, width), :]], axis=1)
    return jnp.dot(lhs_ref[...], rhs, preferred_element_type=F32)


def first_body(row, guest, left, own_ref, head_ref, part_ref, host_ref, *refs):
    term_ref, lhs_ref = refs[-2:]
    whole = host_ref.shape[1] - TILE
    count = part_ref.shape[0]
    last = ending(host_ref[:, pl.ds(whole, TILE)], guest, left)
    part = jnp.concatenate([head_ref[pl.ds(row, count), :], part_ref[:, pl.ds(0, whole)], last], axis=1)
    term_ref[...] = correlate(part, own_ref, lhs_ref).astype(BF16)


def second_body(
    given, before, row, skip, guest, final, seg_len, meta_ref, own_ref, part_ref, host_ref, mark_ref, term_ref, *refs
):
    lhs_ref, sem, gate = refs[-3:]
    count, width = host_ref.shape
    chans = own_ref.shape[1]
    outs = []
    if before:
        prior_ref = refs[0]
        out_ref = refs[given]
        target = out_ref.at[pl.ds((row - before) * LAGS, before * LAGS)]
        outs.append(pltpu.make_async_copy(prior_ref, target, sem.at[0]))
        outs[-1].start()
        pl.semaphore_signal(gate, 1)
        pl.semaphore_wait(gate, 1)
    done_ref = refs[-4]
    tile = host_ref[:, pl.ds(width - TILE, TILE)]
    here = meta_ref[pl.ds(0, count), :] * mark_ref[pl.ds(0, count), pl.ds(mark_ref.shape[1] - TILE, TILE)].astype(F32)
    there = own_ref[pl.ds(width + HALF, count), :].astype(F32) * tile.astype(F32)
    here = here[:, TILE - 1 :]
    there = there[:, TILE - 1 :]
    scale = 1.0 / (jnp.maximum(here + there, 1.0) * math.sqrt(seg_len))
    here = jnp.broadcast_to(here * scale, (count, chans))
    there = jnp.broadcast_to(there * scale, (count, chans))
    last = ending(tile, guest, seg_len % TILE)
    part = jnp.concatenate([part_ref[:, pl.ds(0, width - TILE)], last], axis=1)
    terms = correlate(part, own_ref, lhs_ref).astype(BF16).astype(F32)
    slab = 8
    for low in range(0, count, slab):
        at = skip + low
        pace = term_ref.shape[0] // HALF
        for high in range(2):
            lanes = pl.ds(high * chans, chans)
            for first in range(0, HALF, 8):
                tiles = []
                for lag in range(first, first + 8):
                    line = lag * count + low
                    mine = terms[line : line + slab, high * chans : (high + 1) * chans]
                    held = term_ref[pl.ds(at + lag * pace, slab), lanes].astype(F32)
                    tiles.append(mine * there[low : low + slab] + held * here[low : low + slab])
                turned = jnp.transpose(jnp.stack(tiles, 0), (1, 0, 2))
                for one in range(slab):
                    spot = (low + one) * LAGS + high * HALF + first
                    done_ref[pl.ds(spot, 8), :] = turned[one]
        if final:
            source = done_ref.at[pl.ds(low * LAGS, slab * LAGS)]
            target = out_ref.at[pl.ds((row + low) * LAGS, slab * LAGS)]
            outs.append(pltpu.make_async_copy(source, target, sem.at[1 + low // slab]))
            outs[-1].start()
    for out in outs:
        out.wait()


def body(records, assign, plan, seg_mask):
    chans, seg_count, seg_len = records.shape
    blocks = lax.axis_size("chan")
    half = chans // lax.axis_size("win")
    width = -(-(seg_len + LAGS) // (2 * TILE)) * 2 * TILE
    if width - TILE != seg_len // TILE * TILE or seg_len % TILE > TILE // 2:
        raise ValueError("segment length")
    win = lax.axis_index("win").astype(jnp.int32).reshape(1)
    rec = records.reshape(chans, seg_count * seg_len).T
    slots = assign.reshape(1, chans)
    nears = [count for side, count in ORDER if side == "near"]
    fars = [count for side, count in ORDER if side == "far"]
    shape = jax.ShapeDtypeStruct
    head = width // (4 * TILE) * 2 * TILE
    near_prep = pl.pallas_call(
        near_body,
        out_shape=(
            shape((half, head), BF16),
            shape((head, chans), BF16),
            shape((chans, chans), BF16),
            shape((chans, chans), BF16),
        ),
        in_specs=[SMEM, HBM, HBM],
        out_specs=(VMEM,) * 4,
        scratch_shapes=[
            pltpu.VMEM((chans, chans), F32),
            pltpu.VMEM((1, chans), jnp.int32),
            pltpu.SemaphoreType.DMA((2,)),
        ],
        compiler_params=NEAR_PARAMS,
        cost_estimate=pl.CostEstimate(flops=1 << 26, bytes_accessed=1 << 20, transcendentals=0),
        name="near_prep",
    )
    rest_prep = pl.pallas_call(
        lambda *refs: rest_body(len(nears), *refs),
        out_shape=(shape((width + HALF + 16, chans), BF16), shape((16, 128), F32))
        + tuple(shape((count, width - head - at % 2 * TILE), BF16) for at, count in enumerate(nears))
        + tuple(shape((count, width - at % 2 * TILE), BF16) for at, count in enumerate(fars)),
        in_specs=[SMEM, HBM] + [VMEM] * 3,
        out_specs=(VMEM,) * (len(ORDER) + 2),
        scratch_shapes=[
            pltpu.VMEM((width - head, chans), BF16),
            pltpu.SemaphoreType.DMA((1,)),
            pltpu.SemaphoreType.REGULAR,
        ],
        compiler_params=PARAMS,
        cost_estimate=pl.CostEstimate(flops=1 << 27, bytes_accessed=1 << 20, transcendentals=0),
        name="rest_prep",
    )
    rows = GROUP * HALF
    flops = 2 * rows * width * 2 * chans
    lhs = pltpu.VMEM((rows, width), BF16)

    def first(row, guest, *args):
        count = args[2].shape[0]
        return pl.pallas_call(
            lambda *refs: first_body(row, guest, seg_len % TILE, *refs),
            out_shape=shape((count * HALF, 2 * chans), BF16),
            in_specs=[VMEM] * 4 + [ANY] * (len(args) - 4),
            out_specs=VMEM,
            scratch_shapes=[pltpu.VMEM((count * HALF, width), BF16)],
            compiler_params=PARAMS,
            cost_estimate=pl.CostEstimate(
                flops=flops * count // GROUP, bytes_accessed=1 << 20, transcendentals=0
            ),
            name="first",
        )(*args)

    def second(before, row, skip, guest, meta, other, part, host, mark, terms, done, out, after):
        count = part.shape[0]
        final = row + count == half
        total = shape((half * LAGS, chans), F32)
        held = shape((count * LAGS, chans), F32)
        scratch = [
            pltpu.VMEM((count * HALF, width), BF16),
            pltpu.SemaphoreType.DMA((3,)),
            pltpu.SemaphoreType.REGULAR,
        ]
        if final:
            extra = dict(out_shape=(total,), out_specs=(ANY,))
            scratch = [pltpu.VMEM(held.shape, F32)] + scratch
        elif before:
            extra = dict(out_shape=(total, held), out_specs=(ANY, VMEM))
        else:
            extra = dict(out_shape=(held,), out_specs=(VMEM,))
        given = len(done) + len(out) + len(after)
        return pl.pallas_call(
            lambda *refs: second_body(given, before, row, skip, guest, final, seg_len, *refs),
            in_specs=[VMEM] * (6 + len(done)) + [ANY] * (len(out) + len(after)),
            scratch_shapes=scratch,
            input_output_aliases={7: 0} if out else {},
            compiler_params=PARAMS,
            cost_estimate=pl.CostEstimate(
                flops=flops * count // GROUP, bytes_accessed=1 << 20, transcendentals=0
            ),
            name="second",
            **extra,
        )(meta, other, part, host, mark, terms, *done, *out, *after)

    def exchange(bit):
        straight = []
        crossed = []
        for low in range(blocks):
            for core in range(2):
                straight.append((low * 2 + core, (low ^ 1 << bit) * 2 + core))
                crossed.append((low * 2 + core, (low ^ 1 << bit) * 2 + 1 - core))

        def run(head, pad, turned, pick, rec, flags):
            own, meta, *pieces = rest_prep(flags, rec, pad, turned, pick)
            opening = lax.ppermute(head, ("chan", "win"), straight)
            sent = {"near": pieces[: len(nears)], "far": pieces[len(nears) :]}
            routes = {"near": straight, "far": crossed}
            came = {"near": [], "far": []}
            for at, (side, _) in enumerate(ORDER):
                one = sent[side][len(came[side])]
                came[side].append(lax.ppermute(one, ("chan", "win"), routes[side]))
            other = lax.ppermute(own, "win", [(0, 1), (1, 0)])
            terms = []
            starts = [sum(nears[:at]) for at in range(len(nears))]
            done = out = after = ()
            before = row = taken = 0
            for side, count in ORDER:
                if side == "near":
                    at = len(terms)
                    guest = at % 2
                    parts = (came["near"][at], came["near"][at - guest])
                    terms.append(first(starts[at], guest, own, opening, *parts, *after, *done[:1]))
                    after = (terms[-1],)
                    continue
                home = max(at for at in range(len(nears)) if starts[at] <= row)
                after = after[: after != () and after[0] is not terms[home]]
                guest = taken % 2
                parts = (came["far"][taken], came["far"][taken - guest])
                skip = row - starts[home]
                result = second(
                    before, row, skip, guest, meta, other, *parts, came["near"][0], terms[home], done, out, after
                )
                out = result[:1] if before else ()
                done = result[-1:]
                after = ()
                before = count
                row += count
                taken += 1
            return out[0]

        return run

    digits = blocks.bit_length() - 1
    held = near_prep(win, rec, slots)
    branches = [exchange(bit) for bit in range(digits)]
    out = lax.switch(plan[0], branches, *held, rec, seg_mask)
    return jnp.transpose(out.reshape(half, LAGS, chans), (2, 0, 1))[None]


def solution(mesh):
    placed = (P(("days", "chan"), "win", None), P("chan"), P(), P(("days", "chan"), "win"))
    return jax.shard_map(
        body, mesh=mesh, in_specs=placed, out_specs=P("days", "chan", "win", None), check_vma=False
    )
```

```python
import math

import jax
import jax.numpy as jnp
from jax import lax
from jax.experimental import pallas as pl
from jax.experimental.pallas import tpu as pltpu
from jax.sharding import PartitionSpec as P


LAGS = 64
HALF = LAGS // 2
GROUP = 16
TILE = 128
ORDER = (('near', 32), ('near', 32), ('far', 16), ('far', 16), ('far', 16), ('far', 16))
BF16 = jnp.bfloat16
F32 = jnp.float32
PARAMS = pltpu.CompilerParams(vmem_limit_bytes=24 * 1024 * 1024)

NEAR_PARAMS = pltpu.CompilerParams(vmem_limit_bytes=62 * 1024 * 1024)
SMEM = pl.BlockSpec(memory_space=pltpu.SMEM)
VMEM = pl.BlockSpec(memory_space=pltpu.VMEM)
ANY = pl.BlockSpec(memory_space=pl.ANY)
HBM = pl.BlockSpec(memory_space=pltpu.HBM)


def turn(rows, times_ref):
    return lax.dot_general(
        rows, times_ref[...], (((1,), (1,)), ((), ())), preferred_element_type=F32
    ).astype(BF16)


def near_body(win_ref, rec_ref, assign_ref, head_ref, times_ref, rows_ref, pick_ref, turn_ref, slot_ref, sem):
    chans = rec_ref.shape[1]
    half = chans // 2
    slots = pltpu.make_async_copy(assign_ref, slot_ref, sem.at[0])
    load = pltpu.make_async_copy(rec_ref.at[pl.ds(0, times_ref.shape[0])], times_ref, sem.at[1])
    slots.start()
    load.start()
    slots.wait()
    source = lax.broadcasted_iota(jnp.int32, (chans, chans), 0)
    pick = jnp.where(source == slot_ref[...], 1.0, 0.0)
    pick_ref[...] = pick.astype(BF16)
    turn_ref[...] = pick.T
    near = pl.multiple_of(win_ref[0] * half, half)
    far = pl.multiple_of((1 - win_ref[0]) * half, half)
    rows = turn_ref[pl.ds(near, half), :].astype(BF16)
    rows_ref[pl.ds(0, half), :] = rows
    rows_ref[pl.ds(half, half), :] = turn_ref[pl.ds(far, half), :].astype(BF16)
    load.wait()
    head_ref[...] = turn(rows, times_ref)


def rest_body(nears, mask_ref, rec_ref, times_ref, rows_ref, pick_ref, own_ref, meta_ref, *refs):
    out_refs = refs[:-3]
    tail_ref, sem, gate = refs[-3:]
    seg_len, chans = rec_ref.shape
    head = times_ref.shape[0]
    rest = tail_ref.shape[0]
    half = chans // 2
    count = seg_len - head
    load = pltpu.make_async_copy(
        rec_ref.at[pl.ds(head, count)], tail_ref.at[pl.ds(0, count)], sem.at[0]
    )
    load.start()
    pl.semaphore_signal(gate, 1)
    pl.semaphore_wait(gate, 1)
    tail_ref[pl.ds(count, rest - count), :] = jnp.zeros((rest - count, chans), BF16)
    mask = mask_ref[0, 0].astype(F32)
    meta_ref[...] = jnp.full(meta_ref.shape, mask, F32)
    early = turn(rows_ref[pl.ds(half, half), :], times_ref)
    at = 0
    for out_ref in out_refs[nears:]:
        out_ref[:, pl.ds(0, head)] = early[at : at + out_ref.shape[0]]
        at += out_ref.shape[0]
    own_ref[pl.ds(0, HALF), :] = jnp.zeros((HALF, chans), BF16)
    own_ref[pl.ds(HALF, head), :] = jnp.dot(
        times_ref[...], pick_ref[...], preferred_element_type=F32
    ).astype(BF16)
    own_ref[pl.ds(HALF + head + rest, 16), :] = jnp.full((16, chans), mask, F32).astype(BF16)
    load.wait()
    late = turn(rows_ref[...], tail_ref)
    whole = rest - TILE
    at = 0
    for out_ref in out_refs:
        count, width = out_ref.shape
        host = width % (2 * TILE) == 0
        start = width - rest if host else width - whole
        out_ref[:, pl.ds(start, whole)] = late[at : at + count, :whole]
        if host:
            lane = lax.broadcasted_iota(jnp.int32, (count, TILE), 1)
            mine = late[at : at + count, whole:].astype(F32)
            guest = pltpu.roll(late[at + count : at + 2 * count, whole:].astype(F32), TILE // 2, 1)
            ending = jnp.where(lane == TILE - 1, mask, jnp.where(lane < TILE // 2, mine, guest))
            out_ref[:, pl.ds(width - TILE, TILE)] = ending.astype(BF16)
        at += count
    own_ref[pl.ds(HALF + head, rest), :] = jnp.dot(
        tail_ref[...], pick_ref[...], preferred_element_type=F32
    ).astype(BF16)


def ending(tile, guest, left):
    tile = tile.astype(F32)
    if guest:
        tile = pltpu.roll(tile, TILE // 2, 1)
    lane = lax.broadcasted_iota(jnp.int32, tile.shape, 1)
    return jnp.where(lane < left, tile, 0.0).astype(BF16)


def correlate(part, own_ref, lhs_ref):
    count, width = part.shape
    for lag in range(HALF):
        lhs_ref[pl.ds(lag * count, count), :] = pltpu.roll(part, HALF - lag, 1)
    rhs = jnp.concatenate([own_ref[pl.ds(HALF, width), :], own_ref[pl.ds(0, width), :]], axis=1)
    return jnp.dot(lhs_ref[...], rhs, preferred_element_type=F32)


def first_body(row, guest, left, own_ref, head_ref, part_ref, host_ref, *refs):
    term_ref, lhs_ref = refs[-2:]
    whole = host_ref.shape[1] - TILE

    def step(at, carry):
        rows = pl.ds(pl.multiple_of(at * GROUP, GROUP), GROUP)
        early = head_ref[pl.ds(pl.multiple_of(row + at * GROUP, GROUP), GROUP), :]
        last = ending(host_ref[rows, pl.ds(whole, TILE)], guest, left)
        part = jnp.concatenate([early, part_ref[rows, pl.ds(0, whole)], last], axis=1)
        terms = correlate(part, own_ref, lhs_ref).astype(BF16)
        term_ref[pl.ds(pl.multiple_of(at * GROUP * HALF, GROUP), GROUP * HALF), :] = terms
        return carry

    lax.fori_loop(0, part_ref.shape[0] // GROUP, step, 0)


def second_body(
    given, before, row, skip, guest, final, seg_len, meta_ref, own_ref, part_ref, host_ref, mark_ref, term_ref, *refs
):
    lhs_ref, sem, gate = refs[-3:]
    count, width = host_ref.shape
    chans = own_ref.shape[1]
    outs = []
    if before:
        prior_ref = refs[0]
        out_ref = refs[given]
        target = out_ref.at[pl.ds((row - before) * LAGS, before * LAGS)]
        outs.append(pltpu.make_async_copy(prior_ref, target, sem.at[0]))
        outs[-1].start()
        pl.semaphore_signal(gate, 1)
        pl.semaphore_wait(gate, 1)
    done_ref = refs[-4]
    tile = host_ref[:, pl.ds(width - TILE, TILE)]
    here = meta_ref[pl.ds(0, count), :] * mark_ref[pl.ds(0, count), pl.ds(mark_ref.shape[1] - TILE, TILE)].astype(F32)
    there = own_ref[pl.ds(width + HALF, count), :].astype(F32) * tile.astype(F32)
    here = here[:, TILE - 1 :]
    there = there[:, TILE - 1 :]
    scale = 1.0 / (jnp.maximum(here + there, 1.0) * math.sqrt(seg_len))
    here = jnp.broadcast_to(here * scale, (count, chans))
    there = jnp.broadcast_to(there * scale, (count, chans))
    last = ending(tile, guest, seg_len % TILE)
    part = jnp.concatenate([part_ref[:, pl.ds(0, width - TILE)], last], axis=1)
    terms = correlate(part, own_ref, lhs_ref).astype(BF16).astype(F32)
    slab = 8
    for low in range(0, count, slab):
        at = skip + low
        held_at = at // GROUP * GROUP * HALF + at % GROUP
        for high in range(2):
            lanes = pl.ds(high * chans, chans)
            for first in range(0, HALF, 8):
                tiles = []
                for lag in range(first, first + 8):
                    line = lag * count + low
                    mine = terms[line : line + slab, high * chans : (high + 1) * chans]
                    held = term_ref[pl.ds(held_at + lag * GROUP, slab), lanes].astype(F32)
                    tiles.append(mine * there[low : low + slab] + held * here[low : low + slab])
                turned = jnp.transpose(jnp.stack(tiles, 0), (1, 0, 2))
                for one in range(slab):
                    spot = (low + one) * LAGS + high * HALF + first
                    done_ref[pl.ds(spot, 8), :] = turned[one]
        if final:
            source = done_ref.at[pl.ds(low * LAGS, slab * LAGS)]
            target = out_ref.at[pl.ds((row + low) * LAGS, slab * LAGS)]
            outs.append(pltpu.make_async_copy(source, target, sem.at[1 + low // slab]))
            outs[-1].start()
    for out in outs:
        out.wait()


def body(records, assign, plan, seg_mask):
    chans, seg_count, seg_len = records.shape
    blocks = lax.axis_size("chan")
    half = chans // lax.axis_size("win")
    width = -(-(seg_len + LAGS) // (2 * TILE)) * 2 * TILE
    if width - TILE != seg_len // TILE * TILE or seg_len % TILE > TILE // 2:
        raise ValueError("segment length")
    win = lax.axis_index("win").astype(jnp.int32).reshape(1)
    rec = records.reshape(chans, seg_count * seg_len).T
    slots = assign.reshape(1, chans)
    nears = [count for side, count in ORDER if side == "near"]
    fars = [count for side, count in ORDER if side == "far"]
    shape = jax.ShapeDtypeStruct
    head = width // (4 * TILE) * 2 * TILE
    near_prep = pl.pallas_call(
        near_body,
        out_shape=(
            shape((half, head), BF16),
            shape((head, chans), BF16),
            shape((chans, chans), BF16),
            shape((chans, chans), BF16),
        ),
        in_specs=[SMEM, HBM, HBM],
        out_specs=(VMEM,) * 4,
        scratch_shapes=[
            pltpu.VMEM((chans, chans), F32),
            pltpu.VMEM((1, chans), jnp.int32),
            pltpu.SemaphoreType.DMA((2,)),
        ],
        compiler_params=NEAR_PARAMS,
        cost_estimate=pl.CostEstimate(flops=1 << 26, bytes_accessed=1 << 20, transcendentals=0),
        name="near_prep",
    )
    rest_prep = pl.pallas_call(
        lambda *refs: rest_body(len(nears), *refs),
        out_shape=(shape((width + HALF + 16, chans), BF16), shape((16, 128), F32))
        + tuple(shape((count, width - head - at % 2 * TILE), BF16) for at, count in enumerate(nears))
        + tuple(shape((count, width - at % 2 * TILE), BF16) for at, count in enumerate(fars)),
        in_specs=[SMEM, HBM] + [VMEM] * 3,
        out_specs=(VMEM,) * (len(ORDER) + 2),
        scratch_shapes=[
            pltpu.VMEM((width - head, chans), BF16),
            pltpu.SemaphoreType.DMA((1,)),
            pltpu.SemaphoreType.REGULAR,
        ],
        compiler_params=PARAMS,
        cost_estimate=pl.CostEstimate(flops=1 << 27, bytes_accessed=1 << 20, transcendentals=0),
        name="rest_prep",
    )
    rows = GROUP * HALF
    flops = 2 * rows * width * 2 * chans
    lhs = pltpu.VMEM((rows, width), BF16)

    def first(row, guest, *args):
        count = args[2].shape[0]
        return pl.pallas_call(
            lambda *refs: first_body(row, guest, seg_len % TILE, *refs),
            out_shape=shape((count * HALF, 2 * chans), BF16),
            in_specs=[VMEM] * 4 + [ANY] * (len(args) - 4),
            out_specs=VMEM,
            scratch_shapes=[lhs],
            compiler_params=PARAMS,
            cost_estimate=pl.CostEstimate(
                flops=flops * count // GROUP, bytes_accessed=1 << 20, transcendentals=0
            ),
            name="first",
        )(*args)

    def second(before, row, skip, guest, meta, other, part, host, mark, terms, done, out, after):
        count = part.shape[0]
        final = row + count == half
        total = shape((half * LAGS, chans), F32)
        held = shape((count * LAGS, chans), F32)
        scratch = [
            pltpu.VMEM((count * HALF, width), BF16),
            pltpu.SemaphoreType.DMA((3,)),
            pltpu.SemaphoreType.REGULAR,
        ]
        if final:
            extra = dict(out_shape=(total,), out_specs=(ANY,))
            scratch = [pltpu.VMEM(held.shape, F32)] + scratch
        elif before:
            extra = dict(out_shape=(total, held), out_specs=(ANY, VMEM))
        else:
            extra = dict(out_shape=(held,), out_specs=(VMEM,))
        given = len(done) + len(out) + len(after)
        return pl.pallas_call(
            lambda *refs: second_body(given, before, row, skip, guest, final, seg_len, *refs),
            in_specs=[VMEM] * (6 + len(done)) + [ANY] * (len(out) + len(after)),
            scratch_shapes=scratch,
            input_output_aliases={7: 0} if out else {},
            compiler_params=PARAMS,
            cost_estimate=pl.CostEstimate(
                flops=flops * count // GROUP, bytes_accessed=1 << 20, transcendentals=0
            ),
            name="second",
            **extra,
        )(meta, other, part, host, mark, terms, *done, *out, *after)

    def exchange(bit):
        straight = []
        crossed = []
        for low in range(blocks):
            for core in range(2):
                straight.append((low * 2 + core, (low ^ 1 << bit) * 2 + core))
                crossed.append((low * 2 + core, (low ^ 1 << bit) * 2 + 1 - core))

        def run(head, pad, turned, pick, rec, flags):
            own, meta, *pieces = rest_prep(flags, rec, pad, turned, pick)
            opening = lax.ppermute(head, ("chan", "win"), straight)
            sent = {"near": pieces[: len(nears)], "far": pieces[len(nears) :]}
            routes = {"near": straight, "far": crossed}
            came = {"near": [], "far": []}
            for at, (side, _) in enumerate(ORDER):
                one = sent[side][len(came[side])]
                came[side].append(lax.ppermute(one, ("chan", "win"), routes[side]))
            other = lax.ppermute(own, "win", [(0, 1), (1, 0)])
            terms = []
            starts = [sum(nears[:at]) for at in range(len(nears))]
            done = out = after = ()
            before = row = taken = 0
            for side, count in ORDER:
                if side == "near":
                    at = len(terms)
                    guest = at % 2
                    parts = (came["near"][at], came["near"][at - guest])
                    terms.append(first(starts[at], guest, own, opening, *parts, *after, *done[:1]))
                    after = (terms[-1],)
                    continue
                home = max(at for at in range(len(nears)) if starts[at] <= row)
                after = after[: after != () and after[0] is not terms[home]]
                guest = taken % 2
                parts = (came["far"][taken], came["far"][taken - guest])
                skip = row - starts[home]
                result = second(
                    before, row, skip, guest, meta, other, *parts, came["near"][0], terms[home], done, out, after
                )
                out = result[:1] if before else ()
                done = result[-1:]
                after = ()
                before = count
                row += count
                taken += 1
            return out[0]

        return run

    digits = blocks.bit_length() - 1
    held = near_prep(win, rec, slots)
    branches = [exchange(bit) for bit in range(digits)]
    out = lax.switch(plan[0], branches, *held, rec, seg_mask)
    return jnp.transpose(out.reshape(half, LAGS, chans), (2, 0, 1))[None]


def solution(mesh):
    placed = (P(("days", "chan"), "win", None), P("chan"), P(), P(("days", "chan"), "win"))
    return jax.shard_map(
        body, mesh=mesh, in_specs=placed, out_specs=P("days", "chan", "win", None), check_vma=False
    )
```

```python
import math

import jax
import jax.numpy as jnp
from jax import lax
from jax.experimental import pallas as pl
from jax.experimental.pallas import tpu as pltpu
from jax.sharding import PartitionSpec as P


LAGS = 64
HALF = LAGS // 2
GROUP = 16
TILE = 128
ORDER = (('near', 32), ('near', 32), ('far', 16), ('far', 16), ('far', 16), ('far', 16))
BF16 = jnp.bfloat16
F32 = jnp.float32
PARAMS = pltpu.CompilerParams(vmem_limit_bytes=24 * 1024 * 1024)

NEAR_PARAMS = pltpu.CompilerParams(vmem_limit_bytes=62 * 1024 * 1024)
SMEM = pl.BlockSpec(memory_space=pltpu.SMEM)
VMEM = pl.BlockSpec(memory_space=pltpu.VMEM)
ANY = pl.BlockSpec(memory_space=pl.ANY)
HBM = pl.BlockSpec(memory_space=pltpu.HBM)


def turn(rows, times_ref):
    return lax.dot_general(
        rows, times_ref[...], (((1,), (1,)), ((), ())), preferred_element_type=F32
    ).astype(BF16)


def near_body(win_ref, rec_ref, assign_ref, head_ref, times_ref, rows_ref, pick_ref, turn_ref, slot_ref, sem):
    chans = rec_ref.shape[1]
    half = chans // 2
    slots = pltpu.make_async_copy(assign_ref, slot_ref, sem.at[0])
    load = pltpu.make_async_copy(rec_ref.at[pl.ds(0, times_ref.shape[0])], times_ref, sem.at[1])
    slots.start()
    load.start()
    slots.wait()
    source = lax.broadcasted_iota(jnp.int32, (chans, chans), 0)
    pick = jnp.where(source == slot_ref[...], 1.0, 0.0)
    pick_ref[...] = pick.astype(BF16)
    turn_ref[...] = pick.T
    near = pl.multiple_of(win_ref[0] * half, half)
    far = pl.multiple_of((1 - win_ref[0]) * half, half)
    rows = turn_ref[pl.ds(near, half), :].astype(BF16)
    rows_ref[pl.ds(0, half), :] = rows
    rows_ref[pl.ds(half, half), :] = turn_ref[pl.ds(far, half), :].astype(BF16)
    load.wait()
    head_ref[...] = turn(rows, times_ref)


def rest_body(nears, mask_ref, rec_ref, times_ref, rows_ref, pick_ref, own_ref, meta_ref, *refs):
    out_refs = refs[:-2]
    tail_ref, sem = refs[-2:]
    seg_len, chans = rec_ref.shape
    head = times_ref.shape[0]
    rest = tail_ref.shape[0]
    half = chans // 2
    count = seg_len - head
    load = pltpu.make_async_copy(
        rec_ref.at[pl.ds(head, count)], tail_ref.at[pl.ds(0, count)], sem.at[0]
    )
    load.start()
    tail_ref[pl.ds(count, rest - count), :] = jnp.zeros((rest - count, chans), BF16)
    mask = mask_ref[0, 0].astype(F32)
    meta_ref[...] = jnp.full(meta_ref.shape, mask, F32)
    early = turn(rows_ref[pl.ds(half, half), :], times_ref)
    at = 0
    for out_ref in out_refs[nears:]:
        out_ref[:, pl.ds(0, head)] = early[at : at + out_ref.shape[0]]
        at += out_ref.shape[0]
    own_ref[pl.ds(0, HALF), :] = jnp.zeros((HALF, chans), BF16)
    own_ref[pl.ds(HALF, head), :] = jnp.dot(
        times_ref[...], pick_ref[...], preferred_element_type=F32
    ).astype(BF16)
    own_ref[pl.ds(HALF + head + rest, 16), :] = jnp.full((16, chans), mask, F32).astype(BF16)
    load.wait()
    late = turn(rows_ref[...], tail_ref)
    whole = rest - TILE
    at = 0
    for out_ref in out_refs:
        count, width = out_ref.shape
        host = width % (2 * TILE) == 0
        start = width - rest if host else width - whole
        out_ref[:, pl.ds(start, whole)] = late[at : at + count, :whole]
        if host:
            lane = lax.broadcasted_iota(jnp.int32, (count, TILE), 1)
            mine = late[at : at + count, whole:].astype(F32)
            guest = pltpu.roll(late[at + count : at + 2 * count, whole:].astype(F32), TILE // 2, 1)
            ending = jnp.where(lane == TILE - 1, mask, jnp.where(lane < TILE // 2, mine, guest))
            out_ref[:, pl.ds(width - TILE, TILE)] = ending.astype(BF16)
        at += count
    own_ref[pl.ds(HALF + head, rest), :] = jnp.dot(
        tail_ref[...], pick_ref[...], preferred_element_type=F32
    ).astype(BF16)


def ending(tile, guest, left):
    tile = tile.astype(F32)
    if guest:
        tile = pltpu.roll(tile, TILE // 2, 1)
    lane = lax.broadcasted_iota(jnp.int32, tile.shape, 1)
    return jnp.where(lane < left, tile, 0.0).astype(BF16)


def correlate(part, own_ref, lhs_ref):
    count, width = part.shape
    for lag in range(HALF):
        lhs_ref[pl.ds(lag * count, count), :] = pltpu.roll(part, HALF - lag, 1)
    rhs = jnp.concatenate([own_ref[pl.ds(HALF, width), :], own_ref[pl.ds(0, width), :]], axis=1)
    return jnp.dot(lhs_ref[...], rhs, preferred_element_type=F32)


def first_body(row, guest, left, own_ref, head_ref, part_ref, host_ref, *refs):
    term_ref, lhs_ref = refs[-2:]
    whole = host_ref.shape[1] - TILE

    def step(at, carry):
        rows = pl.ds(pl.multiple_of(at * GROUP, GROUP), GROUP)
        early = head_ref[pl.ds(pl.multiple_of(row + at * GROUP, GROUP), GROUP), :]
        last = ending(host_ref[rows, pl.ds(whole, TILE)], guest, left)
        part = jnp.concatenate([early, part_ref[rows, pl.ds(0, whole)], last], axis=1)
        terms = correlate(part, own_ref, lhs_ref).astype(BF16)
        term_ref[pl.ds(pl.multiple_of(at * GROUP * HALF, GROUP), GROUP * HALF), :] = terms
        return carry

    lax.fori_loop(0, part_ref.shape[0] // GROUP, step, 0)


def second_body(
    given, before, row, skip, guest, final, seg_len, meta_ref, own_ref, part_ref, host_ref, mark_ref, term_ref, *refs
):
    if guest:
        last_ref, *refs = refs
    lhs_ref, sem, gate = refs[-3:]
    count, width = host_ref.shape
    chans = own_ref.shape[1]
    outs = []
    if before:
        prior_ref = refs[0]
        out_ref = refs[given]
        target = out_ref.at[pl.ds((row - before) * LAGS, before * LAGS)]
        outs.append(pltpu.make_async_copy(prior_ref, target, sem.at[0]))
        outs[-1].start()
        pl.semaphore_signal(gate, 1)
        pl.semaphore_wait(gate, 1)
    done_ref = refs[-4]
    tile = host_ref[:, pl.ds(width - TILE, TILE)]
    here = meta_ref[pl.ds(0, count), :] * mark_ref[pl.ds(0, count), pl.ds(mark_ref.shape[1] - TILE, TILE)].astype(F32)
    there = own_ref[pl.ds(width + HALF, count), :].astype(F32) * tile.astype(F32)
    here = here[:, TILE - 1 :]
    there = there[:, TILE - 1 :]
    scale = 1.0 / (jnp.maximum(here + there, 1.0) * math.sqrt(seg_len))
    here = jnp.broadcast_to(here * scale, (count, chans))
    there = jnp.broadcast_to(there * scale, (count, chans))
    if guest:
        last = last_ref[...]
    else:
        last = ending(tile, 0, seg_len % TILE)
        refs[-5][...] = ending(tile, 1, seg_len % TILE)
    part = jnp.concatenate([part_ref[:, pl.ds(0, width - TILE)], last], axis=1)
    terms = correlate(part, own_ref, lhs_ref).astype(BF16).astype(F32)
    slab = 8
    for low in range(0, count, slab):
        at = skip + low
        held_at = at // GROUP * GROUP * HALF + at % GROUP
        for high in range(2):
            lanes = pl.ds(high * chans, chans)
            for first in range(0, HALF, 8):
                tiles = []
                for lag in range(first, first + 8):
                    line = lag * count + low
                    mine = terms[line : line + slab, high * chans : (high + 1) * chans]
                    held = term_ref[pl.ds(held_at + lag * GROUP, slab), lanes].astype(F32)
                    tiles.append(mine * there[low : low + slab] + held * here[low : low + slab])
                turned = jnp.transpose(jnp.stack(tiles, 0), (1, 0, 2))
                for one in range(slab):
                    spot = (low + one) * LAGS + high * HALF + first
                    done_ref[pl.ds(spot, 8), :] = turned[one]
        if final:
            source = done_ref.at[pl.ds(low * LAGS, slab * LAGS)]
            target = out_ref.at[pl.ds((row + low) * LAGS, slab * LAGS)]
            outs.append(pltpu.make_async_copy(source, target, sem.at[1 + low // slab]))
            outs[-1].start()
    for out in outs:
        out.wait()


def body(records, assign, plan, seg_mask):
    chans, seg_count, seg_len = records.shape
    blocks = lax.axis_size("chan")
    half = chans // lax.axis_size("win")
    width = -(-(seg_len + LAGS) // (2 * TILE)) * 2 * TILE
    if width - TILE != seg_len // TILE * TILE or seg_len % TILE > TILE // 2:
        raise ValueError("segment length")
    win = lax.axis_index("win").astype(jnp.int32).reshape(1)
    rec = records.reshape(chans, seg_count * seg_len).T
    slots = assign.reshape(1, chans)
    nears = [count for side, count in ORDER if side == "near"]
    fars = [count for side, count in ORDER if side == "far"]
    shape = jax.ShapeDtypeStruct
    head = width // (4 * TILE) * 2 * TILE
    near_prep = pl.pallas_call(
        near_body,
        out_shape=(
            shape((half, head), BF16),
            shape((head, chans), BF16),
            shape((chans, chans), BF16),
            shape((chans, chans), BF16),
        ),
        in_specs=[SMEM, HBM, HBM],
        out_specs=(VMEM,) * 4,
        scratch_shapes=[
            pltpu.VMEM((chans, chans), F32),
            pltpu.VMEM((1, chans), jnp.int32),
            pltpu.SemaphoreType.DMA((2,)),
        ],
        compiler_params=NEAR_PARAMS,
        cost_estimate=pl.CostEstimate(flops=1 << 26, bytes_accessed=1 << 20, transcendentals=0),
        name="near_prep",
    )
    rest_prep = pl.pallas_call(
        lambda *refs: rest_body(len(nears), *refs),
        out_shape=(shape((width + HALF + 16, chans), BF16), shape((16, 128), F32))
        + tuple(shape((count, width - head - at % 2 * TILE), BF16) for at, count in enumerate(nears))
        + tuple(shape((count, width - at % 2 * TILE), BF16) for at, count in enumerate(fars)),
        in_specs=[SMEM, HBM] + [VMEM] * 3,
        out_specs=(VMEM,) * (len(ORDER) + 2),
        scratch_shapes=[pltpu.VMEM((width - head, chans), BF16), pltpu.SemaphoreType.DMA((1,))],
        compiler_params=PARAMS,
        cost_estimate=pl.CostEstimate(flops=1 << 27, bytes_accessed=1 << 20, transcendentals=0),
        name="rest_prep",
    )
    rows = GROUP * HALF
    flops = 2 * rows * width * 2 * chans
    lhs = pltpu.VMEM((rows, width), BF16)

    def first(row, guest, *args):
        count = args[2].shape[0]
        return pl.pallas_call(
            lambda *refs: first_body(row, guest, seg_len % TILE, *refs),
            out_shape=shape((count * HALF, 2 * chans), BF16),
            in_specs=[VMEM] * 4 + [ANY] * (len(args) - 4),
            out_specs=VMEM,
            scratch_shapes=[lhs],
            compiler_params=PARAMS,
            cost_estimate=pl.CostEstimate(
                flops=flops * count // GROUP, bytes_accessed=1 << 20, transcendentals=0
            ),
            name="first",
        )(*args)

    def second(before, row, skip, last, meta, other, part, host, mark, terms, done, out, after):
        count = part.shape[0]
        final = row + count == half
        total = shape((half * LAGS, chans), F32)
        held = shape((count * LAGS, chans), F32)
        guest = len(last)
        ends = () if guest else (shape((count, TILE), BF16),)
        scratch = [
            pltpu.VMEM((count * HALF, width), BF16),
            pltpu.SemaphoreType.DMA((3,)),
            pltpu.SemaphoreType.REGULAR,
        ]
        if final:
            extra = dict(out_shape=(total,), out_specs=(ANY,))
            scratch = [pltpu.VMEM(held.shape, F32)] + scratch
        elif before:
            extra = dict(out_shape=(total, *ends, held), out_specs=(ANY,) + (VMEM,) * (len(ends) + 1))
        else:
            extra = dict(out_shape=(*ends, held), out_specs=(VMEM,) * (len(ends) + 1))
        given = len(done) + len(out) + len(after)
        return pl.pallas_call(
            lambda *refs: second_body(given, before, row, skip, guest, final, seg_len, *refs),
            in_specs=[VMEM] * (6 + guest + len(done)) + [ANY] * (len(out) + len(after)),
            scratch_shapes=scratch,
            input_output_aliases={7 + guest: 0} if out else {},
            compiler_params=PARAMS,
            cost_estimate=pl.CostEstimate(
                flops=flops * count // GROUP, bytes_accessed=1 << 20, transcendentals=0
            ),
            name="second",
            **extra,
        )(meta, other, part, host, mark, terms, *last, *done, *out, *after)

    def exchange(bit):
        straight = []
        crossed = []
        for low in range(blocks):
            for core in range(2):
                straight.append((low * 2 + core, (low ^ 1 << bit) * 2 + core))
                crossed.append((low * 2 + core, (low ^ 1 << bit) * 2 + 1 - core))

        def run(head, pad, turned, pick, rec, flags):
            own, meta, *pieces = rest_prep(flags, rec, pad, turned, pick)
            opening = lax.ppermute(head, ("chan", "win"), straight)
            sent = {"near": pieces[: len(nears)], "far": pieces[len(nears) :]}
            routes = {"near": straight, "far": crossed}
            came = {"near": [], "far": []}
            for at, (side, _) in enumerate(ORDER):
                one = sent[side][len(came[side])]
                came[side].append(lax.ppermute(one, ("chan", "win"), routes[side]))
            other = lax.ppermute(own, "win", [(0, 1), (1, 0)])
            terms = []
            starts = [sum(nears[:at]) for at in range(len(nears))]
            done = out = after = last = ()
            before = row = taken = 0
            for side, count in ORDER:
                if side == "near":
                    at = len(terms)
                    guest = at % 2
                    parts = (came["near"][at], came["near"][at - guest])
                    terms.append(first(starts[at], guest, own, opening, *parts, *after, *done[:1]))
                    after = (terms[-1],)
                    continue
                home = max(at for at in range(len(nears)) if starts[at] <= row)
                after = after[: after != () and after[0] is not terms[home]]
                guest = taken % 2
                parts = (came["far"][taken], came["far"][taken - guest])
                skip = row - starts[home]
                result = second(
                    before, row, skip, last, meta, other, *parts, came["near"][0], terms[home], done, out, after
                )
                out = result[:1] if before else ()
                done = result[-1:]
                last = () if guest else result[-2:-1]
                after = ()
                before = count
                row += count
                taken += 1
            return out[0]

        return run

    digits = blocks.bit_length() - 1
    held = near_prep(win, rec, slots)
    branches = [exchange(bit) for bit in range(digits)]
    out = lax.switch(plan[0], branches, *held, rec, seg_mask)
    return jnp.transpose(out.reshape(half, LAGS, chans), (2, 0, 1))[None]


def solution(mesh):
    placed = (P(("days", "chan"), "win", None), P("chan"), P(), P(("days", "chan"), "win"))
    return jax.shard_map(
        body, mesh=mesh, in_specs=placed, out_specs=P("days", "chan", "win", None), check_vma=False
    )
```
